128 devices in a mesh: ty: 16 (over z_lo, y, core), tx: 8 (over x, z_hi).
Axes of the slice: x: 4, y: 4, z: 4 (z_hi: 2, z_lo: 2; z = z_hi * 2 + z_lo), core: 2. Of those that a mesh axis runs over, the one named last changes fastest.
Arguments:
- specimen: float32 [2, 8192, 4096], P(None, 'ty', 'tx'), may hold values from -6 to 6
- probe_field: float32 [2, 256, 256], replicated, may hold values from -6 to 6
- intensity: float32 [1024, 256, 256], P(('ty', 'tx')), may hold values from 0.05 to 4
- positions: int32 [1024, 2], P(('ty', 'tx')), may hold values from 0 to 7936, as said below
- occupied_slots: int32 [1024], P(('ty', 'tx')), may hold values from 0 to 1, as said below
Outputs:
- new_specimen: float32 [2, 8192, 4096], P(None, 'ty', 'tx')
- new_probe: float32 [2, 256, 256], replicated
The draws below stay inside these ranges and needn't reach their ends.
Inputs may be any that keep to these rules, and one draw needn't show every extreme that they name: `positions`: slots are grouped by tile, 8 to a tile, tiles in the order of ty then tx. A slot of tile (a, b) has its row between a * 512 - 256 // 2 and a * 512 + 512 - 256 // 2 and its column between b * 512 - 256 // 2 and b * 512 + 512 - 256 // 2, and its window lies inside the object. `occupied_slots`: on each tile the live slots come first; each tile has 1 to 8 live slots, and some tile has all 8.
All inputs are finite; a program needn't handle non-finite values.
Results may differ from the reference program's by a relative error of at most 0.0003.
Values sent between devices are 32-bit elements; how exact they have to be, the bound alone decides.
No kernel may reach another device: no remote copies, remote signals or barrier semaphores. Data moves between devices by JAX's collectives and lax.ppermute only.
A program may use at most 192 MiB of HBM per device.

```python
import math
import jax
import jax.numpy as jnp
from jax import lax

W = 256
TILE = 512
PMAX = 8
ITERS = 2
NR = 8192
NC = 4096
POS_ALL = 1024


def slot_counts(key):
    tile_total = POS_ALL // PMAX
    base_key = jax.random.fold_in(key, 7103)
    key_base, key_full, key_pick = jax.random.split(base_key, 3)
    base = jax.random.randint(key_base, (tile_total,), 1, 5)
    full = jax.random.randint(key_full, (tile_total,), 0, 8) == 0
    chosen = jax.random.randint(key_pick, (), 0, tile_total)
    counts = jnp.where(full | (jnp.arange(tile_total) == chosen), PMAX, base)
    return jnp.minimum(counts, PMAX)


def draw_occupied_slots(key, part):
    counts = slot_counts(key)
    slot_index = jnp.arange(PMAX)
    return (slot_index[None, :] < counts[:, None]).astype(jnp.int32).reshape(POS_ALL)


def draw_positions(key, part):
    columns_of = NC // TILE
    tile_index = jnp.arange(POS_ALL) // PMAX
    tile_row = tile_index // columns_of
    tile_col = tile_index % columns_of
    key_row, key_col = jax.random.split(jax.random.fold_in(key, 9241))
    margin = W // 2
    rows = tile_row * TILE - margin + jax.random.randint(key_row, (POS_ALL,), 0, TILE + 1)
    cols = tile_col * TILE - margin + jax.random.randint(key_col, (POS_ALL,), 0, TILE + 1)
    rows = jnp.clip(rows, 0, NR - W)
    cols = jnp.clip(cols, 0, NC - W)
    last_first = POS_ALL - PMAX
    rows = rows.at[0].set(0).at[last_first].set(NR - W)
    cols = cols.at[0].set(0).at[last_first].set(NC - W)
    return jnp.stack([rows, cols], axis=1).astype(jnp.int32)


def block_levels(rng, extent, shards, smallest, top_value):
    gain = 1.0
    for dim, blocks in shards:
        draws = jax.random.uniform(jax.random.fold_in(jax.random.fold_in(rng, 6), dim), (blocks,), jnp.float32, smallest / len(shards), top_value / len(shards))
        gain = gain * jnp.repeat(jnp.exp(draws), extent[dim] // blocks).reshape((-1,) + (1,) * (len(extent) - 1 - dim))
    return gain


def centred(own_key, shape, width, most, pieces=(), kind=jnp.bfloat16):
    result = width * jax.random.normal(own_key, shape, jnp.float32)
    if pieces:
        result = result * block_levels(own_key, shape, pieces, -0.22, 0.18)
    return jnp.clip(result, -most, most).astype(kind)


def setup_inputs(seed: int = 0) -> dict:
    key_list = jax.random.split(jax.random.key(seed), 6)
    return {
        "specimen": centred(key_list[0], (2, NR, NC), 1.0, 6.0, ((1, 16), (2, 8)), jnp.float32),
        "probe_field": centred(key_list[1], (2, W, W), 1.0, 6.0, (), jnp.float32),
        "intensity": jnp.clip(jnp.exp(math.log(4.0) - 4.3820266 * jax.random.uniform(key_list[2], (POS_ALL, W, W), jnp.float32) ** block_levels(key_list[2], (POS_ALL, W, W), ((0, 128),), -0.2, 0.2)), 0.05, 4.0),
        "positions": draw_positions(jax.random.fold_in(key_list[5], 71), 0),
        "occupied_slots": draw_occupied_slots(jax.random.fold_in(key_list[5], 71), 0),
    }


FLOOR = 0.2
SPECIMEN_REG = 0.5
PROBE_REG = 1.0

def single_sweep(specimen, probe_field, positions, measured_amplitude, slot_occupancy):
    probe_real = probe_field[0]
    probe_imag = probe_field[1]
    anchor = jnp.zeros((), jnp.int32)

    def visit_position(state_tuple, inputs):
        totals, grad_real, grad_imag, density = state_tuple
        corner, measured, weight_live = inputs
        start_row = corner[0].astype(jnp.int32)
        start_col = corner[1].astype(jnp.int32)
        patch = lax.dynamic_slice(specimen, (anchor, start_row, start_col), (2, W, W))
        patch_real = patch[0]
        patch_imag = patch[1]
        exit_real = probe_real * patch_real - probe_imag * patch_imag
        exit_imag = probe_real * patch_imag + probe_imag * patch_real
        spectrum = jnp.fft.fft2(lax.complex(exit_real, exit_imag), norm='ortho')
        spectrum_real = jnp.real(spectrum)
        spectrum_imag = jnp.imag(spectrum)
        magnitude = jnp.sqrt(spectrum_real * spectrum_real + spectrum_imag * spectrum_imag)
        factor = measured / jnp.maximum(magnitude, FLOOR)
        back = jnp.fft.ifft2(lax.complex(spectrum_real * factor, spectrum_imag * factor), norm='ortho')
        diff_real = weight_live * (jnp.real(back) - exit_real)
        diff_imag = weight_live * (jnp.imag(back) - exit_imag)
        contribution = jnp.stack([probe_real * diff_real + probe_imag * diff_imag, probe_real * diff_imag - probe_imag * diff_real, weight_live * (probe_real * probe_real + probe_imag * probe_imag)])
        region = lax.dynamic_slice(totals, (anchor, start_row, start_col), (3, W, W))
        totals = lax.dynamic_update_slice(totals, region + contribution, (anchor, start_row, start_col))
        grad_real = grad_real + patch_real * diff_real + patch_imag * diff_imag
        grad_imag = grad_imag + patch_real * diff_imag - patch_imag * diff_real
        density = density + weight_live * (patch_real * patch_real + patch_imag * patch_imag)
        return ((totals, grad_real, grad_imag, density), None)
    starting_state = (jnp.zeros((3,) + specimen.shape[1:], specimen.dtype), jnp.zeros(probe_real.shape, specimen.dtype), jnp.zeros(probe_real.shape, specimen.dtype), jnp.zeros(probe_real.shape, specimen.dtype))
    converged_state, unused_value = lax.scan(visit_position, starting_state, (positions, measured_amplitude, slot_occupancy))
    totals, grad_real, grad_imag, density = converged_state
    new_specimen = specimen + totals[:2] / (totals[2] + SPECIMEN_REG)
    new_probe = probe_field + jnp.stack([grad_real, grad_imag]) / (density + PROBE_REG)
    return (new_specimen, new_probe)

def reference(specimen, probe_field, intensity, positions, occupied_slots):
    measured_amplitude = jnp.sqrt(intensity)
    slot_occupancy = occupied_slots.astype(specimen.dtype)
    for iteration in range(ITERS):
        specimen, probe_field = single_sweep(specimen, probe_field, positions, measured_amplitude, slot_occupancy)
    return (specimen, probe_field)
```

```python
import functools
import math

import jax
import jax.numpy as jnp
import numpy as np
from jax import lax
from jax.experimental import pallas as pl
from jax.experimental.pallas import tpu as pltpu
from jax.sharding import PartitionSpec as P

FLOOR = 0.2
SPECIMEN_REG = 0.5
PROBE_REG = 1.0

W = 256
H = W // 2
TILE = 512
EXT = TILE + 2 * H
SLOTS = 8
LANES = 128
EXT_TILES = EXT // LANES
BOTH = ("ty", "tx")
F32 = jnp.float32
BF16 = jnp.bfloat16
VMEM = pl.BlockSpec(memory_space=pltpu.VMEM)
SMEM = pl.BlockSpec(memory_space=pltpu.SMEM)


def dft_tables():
    j = np.arange(H)[:, None]
    m = np.arange(H)[None, :]
    parts = []
    for odd in (0, 1):
        phase = -2.0 * np.pi * ((m * (2 * j + odd)) % W) / W
        re, im = np.cos(phase) / math.sqrt(W), np.sin(phase) / math.sqrt(W)
        full = np.block([[re, -im], [im, re]])
        for mat in (full, full.T):
            hi = mat.astype(jnp.bfloat16)
            lo = (mat - hi.astype(np.float64)).astype(jnp.bfloat16)
            parts.append(np.stack([hi, lo]))
    return np.stack(parts)


def column_order():
    pick = np.zeros((W, W), np.float32)
    for k in range(H):
        pick[2 * k, k] = 1.0
        pick[2 * k + 1, H + k] = 1.0
    return pick.astype(jnp.bfloat16)


def split2(x):
    hi = x.astype(BF16)
    return hi, (x - hi.astype(F32)).astype(BF16)


def dot(a, b):
    return jnp.dot(a, b, preferred_element_type=F32)


def split3(x):
    hi = x.astype(BF16)
    return (hi,) + split2(x - hi.astype(F32))


def prep_kernel(intensity, pick, pick_t, amp):
    def slot(p, carry):
        hi, mid, lo = split3(jnp.sqrt(intensity[p]))
        x = dot(lo, pick[...]) + dot(mid, pick[...]) + dot(hi, pick[...])
        hi, mid, lo = split3(x)
        amp[p] = dot(pick_t[...], lo) + dot(pick_t[...], mid) + dot(pick_t[...], hi)
        return carry

    lax.fori_loop(0, SLOTS, slot, 0)


def prepare(intensity):
    pick = column_order()
    return pl.pallas_call(
        prep_kernel,
        out_shape=jax.ShapeDtypeStruct((SLOTS, W, W), F32),
        in_specs=[VMEM, VMEM, VMEM],
        out_specs=VMEM,
        cost_estimate=pl.CostEstimate(flops=4 * 3 * SLOTS * W**3, bytes_accessed=16 * SLOTS * W * W, transcendentals=SLOTS * W * W),
        name="amplitudes",
    )(intensity, jnp.asarray(pick), jnp.asarray(pick.T))


def sweep_kernel(
    corners, alive, tile, left, right, top, bottom, probe, amp, tables,
    u_top, u_mid, u_bottom, packed,
    ext, total, window, exit_wave, grads, a_hi, a_lo, wide,
):
    ext[:, 0, H : H + TILE, :] = left[...]
    ext[:, EXT_TILES - 1, H : H + TILE, :] = right[...]
    for k in range(EXT_TILES):
        cs = pl.ds(k * LANES, LANES)
        if 0 < k < EXT_TILES - 1:
            ext[:, k, H : H + TILE, :] = tile[:, :, pl.ds((k - 1) * LANES, LANES)]
        ext[:, k, 0:H, :] = top[:, :, cs]
        ext[:, k, H + TILE :, :] = bottom[:, :, cs]
    total[...] = jnp.zeros_like(total)
    grads[...] = jnp.zeros_like(grads)
    even, even_t, odd, odd_t = 0, 1, 2, 3
    step = 16
    lane = lax.broadcasted_iota(jnp.int32, (step, LANES), 1)

    def left_dot(t, branch):
        rows = pl.ds(branch * W, W)
        hi, lo = a_hi[rows, :], a_lo[rows, :]
        wide[rows, :] = dot(tables[t, 0], hi) + dot(tables[t, 1], hi) + dot(tables[t, 0], lo)

    def right_dot(t, branch):
        rows = pl.ds(branch * W, W)
        hi, lo = a_hi[rows, :], a_lo[rows, :]
        wide[rows, :] = dot(hi, tables[t, 0]) + dot(hi, tables[t, 1]) + dot(lo, tables[t, 0])

    def put(row, col, value):
        hi, lo = split2(value)
        a_hi[pl.ds(row, step), pl.ds(col, LANES)] = hi
        a_lo[pl.ds(row, step), pl.ds(col, LANES)] = lo

    def slot(p, carry):
        r = corners[p, 0]
        c = corners[p, 1]
        ct = jnp.minimum(c // LANES, EXT_TILES - 3)
        s = c - ct * LANES
        back_turn = lax.rem(LANES - s, LANES)
        forth_turn = lax.rem(s, LANES)

        for i in range(0, H, step):
            waves = []
            for half in (0, 1):
                parts = []
                for plane in (0, 1):
                    turned = [
                        pltpu.roll(ext[plane, ct + k, pl.ds(r + half * H + i, step), :], back_turn, 1)
                        for k in range(3)
                    ]
                    cols = [jnp.where(lane < LANES - s, turned[k], turned[k + 1]) for k in (0, 1)]
                    parts.append(cols)
                rows = pl.ds(half * H + i, step)
                wave = []
                for k in (0, 1):
                    cs = pl.ds(k * LANES, LANES)
                    o_re, o_im = parts[0][k], parts[1][k]
                    p_re, p_im = probe[0, rows, cs], probe[1, rows, cs]
                    w_re = p_re * o_re - p_im * o_im
                    w_im = p_re * o_im + p_im * o_re
                    window[0, rows, cs] = o_re
                    window[1, rows, cs] = o_im
                    exit_wave[0, rows, cs] = w_re
                    exit_wave[1, rows, cs] = w_im
                    wave.append((w_re, w_im))
                waves.append(wave)
            for k in (0, 1):
                for part in (0, 1):
                    x0, x1 = waves[0][k][part], waves[1][k][part]
                    put(part * H + i, k * LANES, x0 + x1)
                    put(W + part * H + i, k * LANES, x0 - x1)
        left_dot(even, 0)
        left_dot(odd, 1)

        for branch in (0, 1):
            for i in range(0, H, step):
                for part in (0, 1):
                    rows = pl.ds(branch * W + part * H + i, step)
                    x0, x1 = wide[rows, 0:LANES], wide[rows, LANES:W]
                    put(branch * H + i, part * LANES, x0 + x1)
                    put(W + branch * H + i, part * LANES, x0 - x1)
        right_dot(even_t, 0)
        right_dot(odd_t, 1)

        for branch in (0, 1):
            for i in range(0, W, step):
                rows = pl.ds(branch * W + i, step)
                z_re, z_im = wide[rows, 0:LANES], wide[rows, LANES:W]
                power = z_re * z_re + z_im * z_im
                factor = amp[p, pl.ds(i, step), pl.ds(branch * LANES, LANES)] * lax.rsqrt(
                    jnp.maximum(power, FLOOR * FLOOR)
                )
                put(branch * W + i, 0, z_re * factor)
                put(branch * W + i, LANES, z_im * factor)
        right_dot(even, 0)
        right_dot(odd, 1)

        for branch in (0, 1):
            for i in range(0, H, step):
                rows_e = pl.ds(branch * H + i, step)
                rows_o = pl.ds(W + branch * H + i, step)
                for part in (0, 1):
                    cs = pl.ds(part * LANES, LANES)
                    x0, x1 = wide[rows_e, cs], wide[rows_o, cs]
                    put(branch * W + part * H + i, 0, x0 + x1)
                    put(branch * W + part * H + i, LANES, x0 - x1)
        left_dot(even_t, 0)
        left_dot(odd_t, 1)

        for i in range(0, H, step):
            for half in (0, 1):
                rows = pl.ds(half * H + i, step)
                turned = [[], []]
                for k in (0, 1):
                    cs = pl.ds(k * LANES, LANES)
                    back = []
                    for part in (0, 1):
                        x0 = wide[pl.ds(part * H + i, step), cs]
                        x1 = wide[pl.ds(W + part * H + i, step), cs]
                        back.append(x0 + x1 if half == 0 else x0 - x1)
                    d_re = back[0] - exit_wave[0, rows, cs]
                    d_im = back[1] - exit_wave[1, rows, cs]
                    o_re, o_im = window[0, rows, cs], window[1, rows, cs]
                    grads[0, rows, cs] += o_re * d_re + o_im * d_im
                    grads[1, rows, cs] += o_re * d_im - o_im * d_re
                    grads[2, rows, cs] += o_re * o_re + o_im * o_im
                    p_re, p_im = probe[0, rows, cs], probe[1, rows, cs]
                    turned[0].append(pltpu.roll(p_re * d_re + p_im * d_im, forth_turn, 1))
                    turned[1].append(pltpu.roll(p_re * d_im - p_im * d_re, forth_turn, 1))
                at = pl.ds(r + half * H + i, step)
                for part in (0, 1):
                    t0, t1 = turned[part]
                    total[part, ct, at, :] += jnp.where(lane >= s, t0, 0.0)
                    total[part, ct + 1, at, :] += jnp.where(lane >= s, t1, t0)
                    total[part, ct + 2, at, :] += jnp.where(lane < s, t1, 0.0)
        return carry

    def visit(p, carry):
        @pl.when(alive[p] != 0)
        def _():
            slot(p, 0)

        return carry

    lax.fori_loop(0, SLOTS, visit, 0)
    for k in range(EXT_TILES):
        cs = pl.ds(k * LANES, LANES)
        u_top[:, :, cs] = total[:, k, 0:H, :]
        u_mid[:, :, cs] = total[:, k, H : H + TILE, :]
        u_bottom[:, :, cs] = total[:, k, H + TILE :, :]
    for k in range(128):
        rows = pl.ds(4 * (k // 2), 4)
        cs = pl.ds((k % 2) * LANES, LANES)
        for plane in range(3):
            packed[k, pl.ds(4 * plane, 4), :] = grads[plane, rows, cs]
        packed[k, pl.ds(12, 4), :] = jnp.zeros((4, LANES), F32)


def sweep(corners, alive, tile, left, right, top, bottom, probe, amp, tables):
    flops = SLOTS * 24 * 2 * W**3
    return pl.pallas_call(
        sweep_kernel,
        out_shape=(
            jax.ShapeDtypeStruct((2, H, EXT), F32),
            jax.ShapeDtypeStruct((2, TILE, EXT), F32),
            jax.ShapeDtypeStruct((2, H, EXT), F32),
            jax.ShapeDtypeStruct((128, 16, LANES), F32),
        ),
        in_specs=[SMEM, SMEM] + [VMEM] * 8,
        out_specs=(VMEM,) * 4,
        scratch_shapes=[
            pltpu.VMEM((2, EXT_TILES, EXT, LANES), F32),
            pltpu.VMEM((2, EXT_TILES, EXT, LANES), F32),
            pltpu.VMEM((2, W, W), F32),
            pltpu.VMEM((2, W, W), F32),
            pltpu.VMEM((3, W, W), F32),
            pltpu.VMEM((2 * W, W), BF16),
            pltpu.VMEM((2 * W, W), BF16),
            pltpu.VMEM((2 * W, W), F32),
        ],
        compiler_params=pltpu.CompilerParams(vmem_limit_bytes=40 << 20),
        cost_estimate=pl.CostEstimate(flops=flops, bytes_accessed=16 << 20, transcendentals=SLOTS * W * W),
        name="sweep",
    )(corners, alive, tile, left, right, top, bottom, probe, amp, tables)


PAD_ROWS = TILE + 2 * W
PAD_TILES = (EXT + 2 * W) // LANES


def light_kernel(spots, probe, weight, density, field):
    density[...] = probe[0] * probe[0] + probe[1] * probe[1]
    field[...] = jnp.zeros_like(field)
    step = 16
    lane = lax.broadcasted_iota(jnp.int32, (step, LANES), 1)

    def spot(q, carry):
        r, c, on = spots[3 * q], spots[3 * q + 1], spots[3 * q + 2]

        @pl.when((on != 0) & (r > 0) & (r < W + TILE) & (c > 0) & (c < W + EXT))
        def _():
            ct = jnp.minimum(c // LANES, PAD_TILES - 3)
            s = c - ct * LANES
            turn = lax.rem(s, LANES)
            for i in range(0, W, step):
                at = pl.ds(r + i, step)
                t0 = pltpu.roll(density[pl.ds(i, step), 0:LANES], turn, 1)
                t1 = pltpu.roll(density[pl.ds(i, step), LANES:W], turn, 1)
                field[ct, at, :] += jnp.where(lane >= s, t0, 0.0)
                field[ct + 1, at, :] += jnp.where(lane >= s, t1, t0)
                field[ct + 2, at, :] += jnp.where(lane < s, t1, 0.0)

        return carry

    lax.fori_loop(0, spots.shape[0] // 3, spot, 0)
    for k in range(EXT_TILES):
        weight[:, pl.ds(k * LANES, LANES)] = 1.0 / (field[W // LANES + k, W : W + TILE, :] + SPECIMEN_REG)


def light(spots, probe):
    return pl.pallas_call(
        light_kernel,
        out_shape=jax.ShapeDtypeStruct((TILE, EXT), F32),
        in_specs=[SMEM, VMEM],
        out_specs=VMEM,
        scratch_shapes=[pltpu.VMEM((W, W), F32), pltpu.VMEM((PAD_TILES, PAD_ROWS, LANES), F32)],
        compiler_params=pltpu.CompilerParams(vmem_limit_bytes=24 << 20),
        cost_estimate=pl.CostEstimate(flops=20 << 20, bytes_accessed=20 << 20, transcendentals=0),
        name="light",
    )(spots, probe)


def shift(value, axis, by):
    length = lax.axis_size(axis)
    pairs = [(i, i + by) for i in range(length) if 0 <= i + by < length]
    return lax.ppermute(value, axis, pairs)


def exchange(value):
    return lax.all_to_all(value, BOTH, 0, 0, tiled=True)


def chunked(plane):
    lead = plane.shape[:-2]
    x = plane.reshape(lead + (64, 4, 2, LANES))
    n = len(lead)
    order = (n, n + 2) + tuple(range(n)) + (n + 1, n + 3)
    return x.transpose(order).reshape((128,) + lead + (4, LANES))


def unchunked(x):
    return x.reshape(64, 2, 2, 4, LANES).transpose(2, 0, 3, 1, 4).reshape(2, W, W)


def probe_step(packed, probe):
    me = lax.axis_index(BOTH)
    mine = exchange(packed.reshape(128 * 16, LANES)).reshape(128, 16, LANES).sum(axis=0)
    own = lax.dynamic_slice(probe, (0, 4 * (me // 2), LANES * (me % 2)), (2, 4, LANES)).reshape(8, LANES)
    denominator = mine[8:12] + PROBE_REG
    new = own + mine[0:8] / jnp.concatenate([denominator, denominator])
    everyone = exchange(jnp.broadcast_to(new, (128, 8, LANES)).reshape(128 * 8, LANES))
    return unchunked(everyone.reshape(128, 2, 4, LANES))


def body(specimen, probe_field, intensity, positions, occupied_slots):
    ty, tx = lax.axis_index("ty"), lax.axis_index("tx")
    row_start = ty * TILE - H
    column_start = tx * TILE - H
    corners = positions - jnp.stack([row_start, column_start])[None, :]
    tables = jnp.asarray(dft_tables())

    left = shift(specimen[:, :, TILE - H :], "tx", 1)
    right = shift(specimen[:, :, :H], "tx", -1)
    amp = prepare(intensity)
    slots = jnp.concatenate([positions, occupied_slots[:, None]], axis=1)
    everywhere = lax.all_gather(slots, BOTH, axis=0, tiled=True).reshape(16, 8, SLOTS, 3)
    around = lax.dynamic_slice(
        jnp.pad(everywhere, ((1, 1), (1, 1), (0, 0), (0, 0))), (ty, tx, 0, 0), (3, 3, SLOTS, 3)
    ).reshape(9 * SLOTS, 3)
    spots = (around - jnp.stack([ty * TILE - W, column_start - W, 0])[None, :]).reshape(-1)
    weight = light(spots, probe_field)
    wide = jnp.concatenate([left, specimen, right], axis=2)
    top = shift(wide[:, TILE - H :, :], "ty", 1)
    bottom = shift(wide[:, :H, :], "ty", -1)

    u_top, u_mid, u_bottom, packed = sweep(
        corners, occupied_slots, specimen, left, right, top, bottom, probe_field, amp, tables
    )
    down = shift(u_bottom, "ty", 1)
    up = shift(u_top, "ty", -1)
    probe_field = probe_step(packed, probe_field)
    u_mid = u_mid.at[:, :H, :].add(down).at[:, TILE - H :, :].add(up)
    from_left = shift(u_mid[:, :, EXT - W :], "tx", 1)
    from_right = shift(u_mid[:, :, :W], "tx", -1)
    u_mid = u_mid.at[:, :, :W].add(from_left).at[:, :, EXT - W :].add(from_right)
    wide = wide + u_mid * weight
    top = shift(wide[:, TILE - H :, :], "ty", 1)
    bottom = shift(wide[:, :H, :], "ty", -1)
    specimen = wide[:, :, H : H + TILE]

    u_top, u_mid, u_bottom, packed = sweep(
        corners, occupied_slots, specimen, wide[:, :, :H], wide[:, :, H + TILE :], top, bottom, probe_field, amp, tables
    )
    down = shift(u_bottom, "ty", 1)
    up = shift(u_top, "ty", -1)
    weight = light(spots, probe_field)
    u_mid = u_mid.at[:, :H, :].add(down).at[:, TILE - H :, :].add(up)
    from_left = shift(u_mid[:, :, EXT - H :], "tx", 1)
    from_right = shift(u_mid[:, :, :H], "tx", -1)
    probe_field = probe_step(packed, probe_field)
    own = u_mid[:, :, H : H + TILE].at[:, :, :H].add(from_left).at[:, :, TILE - H :].add(from_right)
    specimen = specimen + own * weight[:, H : H + TILE]
    return specimen, probe_field


def solution(mesh):
    return jax.shard_map(
        body,
        mesh=mesh,
        in_specs=(
            P(None, "ty", "tx"),
            P(),
            P(BOTH, None, None),
            P(BOTH, None),
            P(BOTH),
        ),
        out_specs=(P(None, "ty", "tx"), P()),
        check_vma=False,
    )
```

```python
import functools
import math

import jax
import jax.numpy as jnp
import numpy as np
from jax import lax
from jax.experimental import pallas as pl
from jax.experimental.pallas import tpu as pltpu
from jax.sharding import PartitionSpec as P

FLOOR = 0.2
SPECIMEN_REG = 0.5
PROBE_REG = 1.0

W = 256
H = W // 2
TILE = 512
EXT = TILE + 2 * H
SLOTS = 8
LANES = 128
EXT_TILES = EXT // LANES
BOTH = ("ty", "tx")
F32 = jnp.float32
BF16 = jnp.bfloat16
VMEM = pl.BlockSpec(memory_space=pltpu.VMEM)
SMEM = pl.BlockSpec(memory_space=pltpu.SMEM)


def dft_tables():
    j = np.arange(H)[:, None]
    m = np.arange(H)[None, :]
    parts = []
    for odd in (0, 1):
        phase = -2.0 * np.pi * ((m * (2 * j + odd)) % W) / W
        re, im = np.cos(phase) / math.sqrt(W), np.sin(phase) / math.sqrt(W)
        full = np.block([[re, -im], [im, re]])
        for mat in (full, full.T):
            hi = mat.astype(jnp.bfloat16)
            lo = (mat - hi.astype(np.float64)).astype(jnp.bfloat16)
            parts.append(np.stack([hi, lo]))
    return np.stack(parts)


def column_order():
    pick = np.zeros((W, W), np.float32)
    for k in range(H):
        pick[2 * k, k] = 1.0
        pick[2 * k + 1, H + k] = 1.0
    return pick.astype(jnp.bfloat16)


def split2(x):
    hi = x.astype(BF16)
    return hi, (x - hi.astype(F32)).astype(BF16)


def dot(a, b):
    return jnp.dot(a, b, preferred_element_type=F32)


def split3(x):
    hi = x.astype(BF16)
    return (hi,) + split2(x - hi.astype(F32))


def prep_kernel(intensity, pick, pick_t, amp):
    def slot(p, carry):
        hi, mid, lo = split3(jnp.sqrt(intensity[p]))
        x = dot(lo, pick[...]) + dot(mid, pick[...]) + dot(hi, pick[...])
        hi, mid, lo = split3(x)
        amp[p] = dot(pick_t[...], lo) + dot(pick_t[...], mid) + dot(pick_t[...], hi)
        return carry

    lax.fori_loop(0, SLOTS, slot, 0)


def prepare(intensity):
    pick = column_order()
    return pl.pallas_call(
        prep_kernel,
        out_shape=jax.ShapeDtypeStruct((SLOTS, W, W), F32),
        in_specs=[VMEM, VMEM, VMEM],
        out_specs=VMEM,
        cost_estimate=pl.CostEstimate(flops=4 * 3 * SLOTS * W**3, bytes_accessed=16 * SLOTS * W * W, transcendentals=SLOTS * W * W),
        name="amplitudes",
    )(intensity, jnp.asarray(pick), jnp.asarray(pick.T))


def sweep_kernel(
    corners, alive, tile, left, right, top, bottom, probe, amp, tables,
    u_top, u_mid, u_bottom, packed,
    ext, total, window, exit_wave, grads, a_hi, a_lo, wide,
):
    ext[:, 0, H : H + TILE, :] = left[...]
    ext[:, EXT_TILES - 1, H : H + TILE, :] = right[...]
    for k in range(EXT_TILES):
        cs = pl.ds(k * LANES, LANES)
        if 0 < k < EXT_TILES - 1:
            ext[:, k, H : H + TILE, :] = tile[:, :, pl.ds((k - 1) * LANES, LANES)]
        ext[:, k, 0:H, :] = top[:, :, cs]
        ext[:, k, H + TILE :, :] = bottom[:, :, cs]
    total[...] = jnp.zeros_like(total)
    grads[...] = jnp.zeros_like(grads)
    even, even_t, odd, odd_t = 0, 1, 2, 3
    step = 16
    lane = lax.broadcasted_iota(jnp.int32, (step, LANES), 1)

    def left_dot(t, branch):
        rows = pl.ds(branch * W, W)
        hi, lo = a_hi[rows, :], a_lo[rows, :]
        wide[rows, :] = dot(tables[t, 0], hi) + dot(tables[t, 1], hi) + dot(tables[t, 0], lo)

    def right_dot(t, branch):
        rows = pl.ds(branch * W, W)
        hi, lo = a_hi[rows, :], a_lo[rows, :]
        wide[rows, :] = dot(hi, tables[t, 0]) + dot(hi, tables[t, 1]) + dot(lo, tables[t, 0])

    def put(row, col, value):
        hi, lo = split2(value)
        a_hi[pl.ds(row, step), pl.ds(col, LANES)] = hi
        a_lo[pl.ds(row, step), pl.ds(col, LANES)] = lo

    def slot(p, carry):
        r = corners[p, 0]
        c = corners[p, 1]
        ct = jnp.minimum(c // LANES, EXT_TILES - 3)
        s = c - ct * LANES
        back_turn = lax.rem(LANES - s, LANES)
        forth_turn = lax.rem(s, LANES)

        for i in range(0, H, step):
            waves = []
            for half in (0, 1):
                parts = []
                for plane in (0, 1):
                    turned = [
                        pltpu.roll(ext[plane, ct + k, pl.ds(r + half * H + i, step), :], back_turn, 1)
                        for k in range(3)
                    ]
                    cols = [jnp.where(lane < LANES - s, turned[k], turned[k + 1]) for k in (0, 1)]
                    parts.append(cols)
                rows = pl.ds(half * H + i, step)
                wave = []
                for k in (0, 1):
                    cs = pl.ds(k * LANES, LANES)
                    o_re, o_im = parts[0][k], parts[1][k]
                    p_re, p_im = probe[0, rows, cs], probe[1, rows, cs]
                    w_re = p_re * o_re - p_im * o_im
                    w_im = p_re * o_im + p_im * o_re
                    window[0, rows, cs] = o_re
                    window[1, rows, cs] = o_im
                    exit_wave[0, rows, cs] = w_re
                    exit_wave[1, rows, cs] = w_im
                    wave.append((w_re, w_im))
                waves.append(wave)
            for k in (0, 1):
                for part in (0, 1):
                    x0, x1 = waves[0][k][part], waves[1][k][part]
                    put(part * H + i, k * LANES, x0 + x1)
                    put(W + part * H + i, k * LANES, x0 - x1)
        left_dot(even, 0)
        left_dot(odd, 1)

        for branch in (0, 1):
            for i in range(0, H, step):
                for part in (0, 1):
                    rows = pl.ds(branch * W + part * H + i, step)
                    x0, x1 = wide[rows, 0:LANES], wide[rows, LANES:W]
                    put(branch * H + i, part * LANES, x0 + x1)
                    put(W + branch * H + i, part * LANES, x0 - x1)
        right_dot(even_t, 0)
        right_dot(odd_t, 1)

        for branch in (0, 1):
            for i in range(0, W, step):
                rows = pl.ds(branch * W + i, step)
                z_re, z_im = wide[rows, 0:LANES], wide[rows, LANES:W]
                power = z_re * z_re + z_im * z_im
                factor = amp[p, pl.ds(i, step), pl.ds(branch * LANES, LANES)] * lax.rsqrt(
                    jnp.maximum(power, FLOOR * FLOOR)
                )
                put(branch * W + i, 0, z_re * factor)
                put(branch * W + i, LANES, z_im * factor)
        right_dot(even, 0)
        right_dot(odd, 1)

        for branch in (0, 1):
            for i in range(0, H, step):
                rows_e = pl.ds(branch * H + i, step)
                rows_o = pl.ds(W + branch * H + i, step)
                for part in (0, 1):
                    cs = pl.ds(part * LANES, LANES)
                    x0, x1 = wide[rows_e, cs], wide[rows_o, cs]
                    put(branch * W + part * H + i, 0, x0 + x1)
                    put(branch * W + part * H + i, LANES, x0 - x1)
        left_dot(even_t, 0)
        left_dot(odd_t, 1)

        for i in range(0, H, step):
            for half in (0, 1):
                rows = pl.ds(half * H + i, step)
                turned = [[], []]
                for k in (0, 1):
                    cs = pl.ds(k * LANES, LANES)
                    back = []
                    for part in (0, 1):
                        x0 = wide[pl.ds(part * H + i, step), cs]
                        x1 = wide[pl.ds(W + part * H + i, step), cs]
                        back.append(x0 + x1 if half == 0 else x0 - x1)
                    d_re = back[0] - exit_wave[0, rows, cs]
                    d_im = back[1] - exit_wave[1, rows, cs]
                    o_re, o_im = window[0, rows, cs], window[1, rows, cs]
                    grads[0, rows, cs] += o_re * d_re + o_im * d_im
                    grads[1, rows, cs] += o_re * d_im - o_im * d_re
                    grads[2, rows, cs] += o_re * o_re + o_im * o_im
                    p_re, p_im = probe[0, rows, cs], probe[1, rows, cs]
                    turned[0].append(pltpu.roll(p_re * d_re + p_im * d_im, forth_turn, 1))
                    turned[1].append(pltpu.roll(p_re * d_im - p_im * d_re, forth_turn, 1))
                at = pl.ds(r + half * H + i, step)
                for part in (0, 1):
                    t0, t1 = turned[part]
                    total[part, ct, at, :] += jnp.where(lane >= s, t0, 0.0)
                    total[part, ct + 1, at, :] += jnp.where(lane >= s, t1, t0)
                    total[part, ct + 2, at, :] += jnp.where(lane < s, t1, 0.0)
        return carry

    def visit(p, carry):
        @pl.when(alive[p] != 0)
        def _():
            slot(p, 0)

        return carry

    lax.fori_loop(0, SLOTS, visit, 0)
    for k in range(EXT_TILES):
        cs = pl.ds(k * LANES, LANES)
        u_top[:, :, cs] = total[:, k, 0:H, :]
        u_mid[:, :, cs] = total[:, k, H : H + TILE, :]
        u_bottom[:, :, cs] = total[:, k, H + TILE :, :]
    for k in range(128):
        rows = pl.ds(4 * (k // 2), 4)
        cs = pl.ds((k % 2) * LANES, LANES)
        for plane in range(3):
            packed[k, pl.ds(4 * plane, 4), :] = grads[plane, rows, cs]
        packed[k, pl.ds(12, 4), :] = jnp.zeros((4, LANES), F32)


def sweep(corners, alive, tile, left, right, top, bottom, probe, amp, tables):
    flops = SLOTS * 24 * 2 * W**3
    return pl.pallas_call(
        sweep_kernel,
        out_shape=(
            jax.ShapeDtypeStruct((2, H, EXT), F32),
            jax.ShapeDtypeStruct((2, TILE, EXT), F32),
            jax.ShapeDtypeStruct((2, H, EXT), F32),
            jax.ShapeDtypeStruct((128, 16, LANES), F32),
        ),
        in_specs=[SMEM, SMEM] + [VMEM] * 8,
        out_specs=(VMEM,) * 4,
        scratch_shapes=[
            pltpu.VMEM((2, EXT_TILES, EXT, LANES), F32),
            pltpu.VMEM((2, EXT_TILES, EXT, LANES), F32),
            pltpu.VMEM((2, W, W), F32),
            pltpu.VMEM((2, W, W), F32),
            pltpu.VMEM((3, W, W), F32),
            pltpu.VMEM((2 * W, W), BF16),
            pltpu.VMEM((2 * W, W), BF16),
            pltpu.VMEM((2 * W, W), F32),
        ],
        compiler_params=pltpu.CompilerParams(vmem_limit_bytes=40 << 20),
        cost_estimate=pl.CostEstimate(flops=flops, bytes_accessed=16 << 20, transcendentals=SLOTS * W * W),
        name="sweep",
    )(corners, alive, tile, left, right, top, bottom, probe, amp, tables)


PAD_ROWS = TILE + 2 * W
PAD_TILES = (EXT + 2 * W) // LANES


def light_kernel(spots, probe, weight, density, field):
    density[...] = probe[0] * probe[0] + probe[1] * probe[1]
    field[...] = jnp.zeros_like(field)
    step = 16
    lane = lax.broadcasted_iota(jnp.int32, (step, LANES), 1)

    def spot(q, carry):
        r, c, on = spots[3 * q], spots[3 * q + 1], spots[3 * q + 2]

        @pl.when((on != 0) & (r > 0) & (r < W + TILE) & (c > 0) & (c < W + EXT))
        def _():
            ct = jnp.minimum(c // LANES, PAD_TILES - 3)
            s = c - ct * LANES
            turn = lax.rem(s, LANES)
            for i in range(0, W, step):
                at = pl.ds(r + i, step)
                t0 = pltpu.roll(density[pl.ds(i, step), 0:LANES], turn, 1)
                t1 = pltpu.roll(density[pl.ds(i, step), LANES:W], turn, 1)
                field[ct, at, :] += jnp.where(lane >= s, t0, 0.0)
                field[ct + 1, at, :] += jnp.where(lane >= s, t1, t0)
                field[ct + 2, at, :] += jnp.where(lane < s, t1, 0.0)

        return carry

    lax.fori_loop(0, spots.shape[0] // 3, spot, 0)
    for k in range(EXT_TILES):
        weight[:, pl.ds(k * LANES, LANES)] = 1.0 / (field[W // LANES + k, W : W + TILE, :] + SPECIMEN_REG)


def light(spots, probe):
    return pl.pallas_call(
        light_kernel,
        out_shape=jax.ShapeDtypeStruct((TILE, EXT), F32),
        in_specs=[SMEM, VMEM],
        out_specs=VMEM,
        scratch_shapes=[pltpu.VMEM((W, W), F32), pltpu.VMEM((PAD_TILES, PAD_ROWS, LANES), F32)],
        compiler_params=pltpu.CompilerParams(vmem_limit_bytes=24 << 20),
        cost_estimate=pl.CostEstimate(flops=20 << 20, bytes_accessed=20 << 20, transcendentals=0),
        name="light",
    )(spots, probe)


def shift(value, axis, by):
    length = lax.axis_size(axis)
    pairs = [(i, i + by) for i in range(length) if 0 <= i + by < length]
    return lax.ppermute(value, axis, pairs)


def exchange(value):
    return lax.all_to_all(value, BOTH, 0, 0, tiled=True)


def chunked(plane):
    lead = plane.shape[:-2]
    x = plane.reshape(lead + (64, 4, 2, LANES))
    n = len(lead)
    order = (n, n + 2) + tuple(range(n)) + (n + 1, n + 3)
    return x.transpose(order).reshape((128,) + lead + (4, LANES))


def unchunked(x):
    return x.reshape(64, 2, 2, 4, LANES).transpose(2, 0, 3, 1, 4).reshape(2, W, W)


def probe_step(packed, probe):
    me = lax.axis_index(BOTH)
    mine = exchange(packed.reshape(128 * 16, LANES)).reshape(128, 16, LANES).sum(axis=0)
    own = lax.dynamic_slice(probe, (0, 4 * (me // 2), LANES * (me % 2)), (2, 4, LANES)).reshape(8, LANES)
    denominator = mine[8:12] + PROBE_REG
    new = own + mine[0:8] / jnp.concatenate([denominator, denominator])
    everyone = exchange(jnp.broadcast_to(new, (128, 8, LANES)).reshape(128 * 8, LANES))
    return unchunked(everyone.reshape(128, 2, 4, LANES))


def body(specimen, probe_field, intensity, positions, occupied_slots):
    ty, tx = lax.axis_index("ty"), lax.axis_index("tx")
    row_start = ty * TILE - H
    column_start = tx * TILE - H
    corners = positions - jnp.stack([row_start, column_start])[None, :]
    tables = jnp.asarray(dft_tables())

    left = shift(specimen[:, :, TILE - H :], "tx", 1)
    right = shift(specimen[:, :, :H], "tx", -1)
    amp = prepare(intensity)
    slots = jnp.concatenate([positions, occupied_slots[:, None]], axis=1)
    line = jnp.stack([shift(slots, "tx", 1), slots, shift(slots, "tx", -1)])
    wide = jnp.concatenate([left, specimen, right], axis=2)
    top = shift(wide[:, TILE - H :, :], "ty", 1)
    bottom = shift(wide[:, :H, :], "ty", -1)
    around = jnp.concatenate([shift(line, "ty", 1), line, shift(line, "ty", -1)]).reshape(9 * SLOTS, 3)
    spots = (around - jnp.stack([ty * TILE - W, column_start - W, 0])[None, :]).reshape(-1)
    weight = light(spots, probe_field)

    u_top, u_mid, u_bottom, packed = sweep(
        corners, occupied_slots, specimen, left, right, top, bottom, probe_field, amp, tables
    )
    down = shift(u_bottom, "ty", 1)
    up = shift(u_top, "ty", -1)
    probe_field = probe_step(packed, probe_field)
    u_mid = u_mid.at[:, :H, :].add(down).at[:, TILE - H :, :].add(up)
    from_left = shift(u_mid[:, :, EXT - W :], "tx", 1)
    from_right = shift(u_mid[:, :, :W], "tx", -1)
    u_mid = u_mid.at[:, :, :W].add(from_left).at[:, :, EXT - W :].add(from_right)
    wide = wide + u_mid * weight
    top = shift(wide[:, TILE - H :, :], "ty", 1)
    bottom = shift(wide[:, :H, :], "ty", -1)
    specimen = wide[:, :, H : H + TILE]

    u_top, u_mid, u_bottom, packed = sweep(
        corners, occupied_slots, specimen, wide[:, :, :H], wide[:, :, H + TILE :], top, bottom, probe_field, amp, tables
    )
    down = shift(u_bottom, "ty", 1)
    up = shift(u_top, "ty", -1)
    weight = light(spots, probe_field)
    u_mid = u_mid.at[:, :H, :].add(down).at[:, TILE - H :, :].add(up)
    from_left = shift(u_mid[:, :, EXT - H :], "tx", 1)
    from_right = shift(u_mid[:, :, :H], "tx", -1)
    probe_field = probe_step(packed, probe_field)
    own = u_mid[:, :, H : H + TILE].at[:, :, :H].add(from_left).at[:, :, TILE - H :].add(from_right)
    specimen = specimen + own * weight[:, H : H + TILE]
    return specimen, probe_field


def solution(mesh):
    return jax.shard_map(
        body,
        mesh=mesh,
        in_specs=(
            P(None, "ty", "tx"),
            P(),
            P(BOTH, None, None),
            P(BOTH, None),
            P(BOTH),
        ),
        out_specs=(P(None, "ty", "tx"), P()),
        check_vma=False,
    )
```

```python
import functools
import math

import jax
import jax.numpy as jnp
import numpy as np
from jax import lax
from jax.experimental import pallas as pl
from jax.experimental.pallas import tpu as pltpu
from jax.sharding import PartitionSpec as P

FLOOR = 0.2
SPECIMEN_REG = 0.5
PROBE_REG = 1.0

W = 256
H = W // 2
TILE = 512
EXT = TILE + 2 * H
SLOTS = 8
LANES = 128
EXT_TILES = EXT // LANES
CHUNKS = 64
BOTH = ("ty", "tx")
F32 = jnp.float32
BF16 = jnp.bfloat16
VMEM = pl.BlockSpec(memory_space=pltpu.VMEM)
SMEM = pl.BlockSpec(memory_space=pltpu.SMEM)


def dft_tables():
    j = np.arange(H)[:, None]
    m = np.arange(H)[None, :]
    parts = []
    for odd in (0, 1):
        phase = -2.0 * np.pi * ((m * (2 * j + odd)) % W) / W
        re, im = np.cos(phase) / math.sqrt(W), np.sin(phase) / math.sqrt(W)
        full = np.block([[re, -im], [im, re]])
        for mat in (full, full.T):
            hi = mat.astype(jnp.bfloat16)
            lo = (mat - hi.astype(np.float64)).astype(jnp.bfloat16)
            parts.append(np.stack([hi, lo]))
    return np.stack(parts)


def column_order():
    pick = np.zeros((W, W), np.float32)
    for k in range(H):
        pick[2 * k, k] = 1.0
        pick[2 * k + 1, H + k] = 1.0
    return pick.astype(jnp.bfloat16)


def split2(x):
    hi = x.astype(BF16)
    return hi, (x - hi.astype(F32)).astype(BF16)


def dot(a, b):
    return jnp.dot(a, b, preferred_element_type=F32)


def split3(x):
    hi = x.astype(BF16)
    return (hi,) + split2(x - hi.astype(F32))


def prep_kernel(intensity, pick, pick_t, amp):
    def slot(p, carry):
        hi, mid, lo = split3(jnp.sqrt(intensity[p]))
        x = dot(lo, pick[...]) + dot(mid, pick[...]) + dot(hi, pick[...])
        hi, mid, lo = split3(x)
        amp[p] = dot(pick_t[...], lo) + dot(pick_t[...], mid) + dot(pick_t[...], hi)
        return carry

    lax.fori_loop(0, SLOTS, slot, 0)


def prepare(intensity):
    pick = column_order()
    return pl.pallas_call(
        prep_kernel,
        out_shape=pltpu.HBM((SLOTS, W, W), F32),
        in_specs=[VMEM, VMEM, VMEM],
        out_specs=VMEM,
        cost_estimate=pl.CostEstimate(flops=4 * 3 * SLOTS * W**3, bytes_accessed=16 * SLOTS * W * W, transcendentals=SLOTS * W * W),
        name="amplitudes",
    )(intensity, jnp.asarray(pick), jnp.asarray(pick.T))


def run_copies(pairs, sems):
    copies = [pltpu.make_async_copy(src, dst, sems.at[n]) for n, (src, dst) in enumerate(pairs)]
    for copy in copies:
        copy.start()
    return copies


def first_loads(refs, ext):
    tile, left, right, top, bottom, corner_top, corner_bottom = refs
    inner, upper, lower = pl.ds(H, TILE), pl.ds(0, H), pl.ds(H + TILE, H)
    last = EXT_TILES - 1
    pairs = [
        (left.at[:, pl.ds(0, TILE)], ext.at[:, 0, inner]),
        (right.at[:, pl.ds(0, TILE)], ext.at[:, last, inner]),
        (corner_top.at[:, 0, pl.ds(0, H)], ext.at[:, 0, upper]),
        (corner_top.at[:, 1, pl.ds(0, H)], ext.at[:, last, upper]),
        (corner_bottom.at[:, 0, pl.ds(0, H)], ext.at[:, 0, lower]),
        (corner_bottom.at[:, 1, pl.ds(0, H)], ext.at[:, last, lower]),
    ]
    for k in range(TILE // LANES):
        cs = pl.ds(k * LANES, LANES)
        pairs.append((tile.at[:, :, cs], ext.at[:, 1 + k, inner]))
        pairs.append((top.at[:, :, cs], ext.at[:, 1 + k, upper]))
        pairs.append((bottom.at[:, :, cs], ext.at[:, 1 + k, lower]))
    return pairs


def later_loads(refs, ext):
    middle, top, bottom = refs
    return [
        (middle, ext.at[:, :, pl.ds(H, TILE)]),
        (top, ext.at[:, :, pl.ds(0, H)]),
        (bottom, ext.at[:, :, pl.ds(H + TILE, H)]),
    ]


FIRST_COPIES = 18
LATER_COPIES = 3


def unpack_probe(halves, probe):
    for h, chunks in enumerate(halves):
        for k in range(CHUNKS):
            rows = pl.ds(h * H + 4 * (k // 2), 4)
            cs = pl.ds((k % 2) * LANES, LANES)
            probe[0, rows, cs] = chunks[k, 0:4, :]
            probe[1, rows, cs] = chunks[k, 4:8, :]


def sweep_kernel(first, corners, alive, *refs):
    n, m = (7, 1) if first else (3, 2)
    objects, probe_in, (amp_in, tables_in) = refs[:n], refs[n : n + m], refs[n + m : n + m + 2]
    rest = refs[n + m + 2 :]
    half = alive[SLOTS]
    u_mid, probe, u_top, u_bottom, s_left, s_right, keep, give = rest[:8]
    total, ext, pack, amp, tables, window, exit_wave, grads, a_hi, a_lo, wide, ext_sems, amp_sems, sems, out_sems, halves = rest[8:]
    loads = first_loads if first else later_loads
    copies = run_copies(loads(objects, ext), ext_sems)
    more = [(tables_in, tables)]
    if first:
        more.append((probe_in[0], probe))
    else:
        more += [(probe_in[0], halves.at[half]), (probe_in[1], halves.at[1 - half])]
    copies += run_copies(more, sems)
    run_copies([(amp_in.at[p], amp.at[p]) for p in range(SLOTS)], amp_sems)
    total[...] = jnp.zeros_like(total)
    grads[...] = jnp.zeros_like(grads)
    even, even_t, odd, odd_t = 0, 1, 2, 3
    step = 16
    lane = lax.broadcasted_iota(jnp.int32, (step, LANES), 1)
    for copy in copies:
        copy.wait()
    if not first:
        unpack_probe((halves.at[0], halves.at[1]), probe)

    def left_dot(t, branch):
        rows = pl.ds(branch * W, W)
        hi, lo = a_hi[rows, :], a_lo[rows, :]
        wide[rows, :] = dot(tables[t, 0], hi) + dot(tables[t, 1], hi) + dot(tables[t, 0], lo)

    def right_dot(t, branch):
        rows = pl.ds(branch * W, W)
        hi, lo = a_hi[rows, :], a_lo[rows, :]
        wide[rows, :] = dot(hi, tables[t, 0]) + dot(hi, tables[t, 1]) + dot(lo, tables[t, 0])

    def put(row, col, value):
        hi, lo = split2(value)
        a_hi[pl.ds(row, step), pl.ds(col, LANES)] = hi
        a_lo[pl.ds(row, step), pl.ds(col, LANES)] = lo

    def slot(p, carry):
        r = corners[p, 0]
        c = corners[p, 1]
        ct = jnp.minimum(c // LANES, EXT_TILES - 3)
        s = c - ct * LANES
        back_turn = lax.rem(LANES - s, LANES)
        forth_turn = lax.rem(s, LANES)

        for i in range(0, H, step):
            waves = []
            for half in (0, 1):
                parts = []
                for plane in (0, 1):
                    turned = [
                        pltpu.roll(ext[plane, ct + k, pl.ds(r + half * H + i, step), :], back_turn, 1)
                        for k in range(3)
                    ]
                    cols = [jnp.where(lane < LANES - s, turned[k], turned[k + 1]) for k in (0, 1)]
                    parts.append(cols)
                rows = pl.ds(half * H + i, step)
                wave = []
                for k in (0, 1):
                    cs = pl.ds(k * LANES, LANES)
                    o_re, o_im = parts[0][k], parts[1][k]
                    p_re, p_im = probe[0, rows, cs], probe[1, rows, cs]
                    w_re = p_re * o_re - p_im * o_im
                    w_im = p_re * o_im + p_im * o_re
                    window[0, rows, cs] = o_re
                    window[1, rows, cs] = o_im
                    exit_wave[0, rows, cs] = w_re
                    exit_wave[1, rows, cs] = w_im
                    wave.append((w_re, w_im))
                waves.append(wave)
            for k in (0, 1):
                for part in (0, 1):
                    x0, x1 = waves[0][k][part], waves[1][k][part]
                    put(part * H + i, k * LANES, x0 + x1)
                    put(W + part * H + i, k * LANES, x0 - x1)
        left_dot(even, 0)
        left_dot(odd, 1)

        for branch in (0, 1):
            for i in range(0, H, step):
                for part in (0, 1):
                    rows = pl.ds(branch * W + part * H + i, step)
                    x0, x1 = wide[rows, 0:LANES], wide[rows, LANES:W]
                    put(branch * H + i, part * LANES, x0 + x1)
                    put(W + branch * H + i, part * LANES, x0 - x1)
        right_dot(even_t, 0)
        right_dot(odd_t, 1)

        for branch in (0, 1):
            for i in range(0, W, step):
                rows = pl.ds(branch * W + i, step)
                z_re, z_im = wide[rows, 0:LANES], wide[rows, LANES:W]
                power = z_re * z_re + z_im * z_im
                factor = amp[p, pl.ds(i, step), pl.ds(branch * LANES, LANES)] * lax.rsqrt(
                    jnp.maximum(power, FLOOR * FLOOR)
                )
                put(branch * W + i, 0, z_re * factor)
                put(branch * W + i, LANES, z_im * factor)
        right_dot(even, 0)
        right_dot(odd, 1)

        for branch in (0, 1):
            for i in range(0, H, step):
                rows_e = pl.ds(branch * H + i, step)
                rows_o = pl.ds(W + branch * H + i, step)
                for part in (0, 1):
                    cs = pl.ds(part * LANES, LANES)
                    x0, x1 = wide[rows_e, cs], wide[rows_o, cs]
                    put(branch * W + part * H + i, 0, x0 + x1)
                    put(branch * W + part * H + i, LANES, x0 - x1)
        left_dot(even_t, 0)
        left_dot(odd_t, 1)

        for i in range(0, H, step):
            for half in (0, 1):
                rows = pl.ds(half * H + i, step)
                turned = [[], []]
                for k in (0, 1):
                    cs = pl.ds(k * LANES, LANES)
                    back = []
                    for part in (0, 1):
                        x0 = wide[pl.ds(part * H + i, step), cs]
                        x1 = wide[pl.ds(W + part * H + i, step), cs]
                        back.append(x0 + x1 if half == 0 else x0 - x1)
                    d_re = back[0] - exit_wave[0, rows, cs]
                    d_im = back[1] - exit_wave[1, rows, cs]
                    o_re, o_im = window[0, rows, cs], window[1, rows, cs]
                    grads[0, rows, cs] += o_re * d_re + o_im * d_im
                    grads[1, rows, cs] += o_re * d_im - o_im * d_re
                    grads[2, rows, cs] += o_re * o_re + o_im * o_im
                    p_re, p_im = probe[0, rows, cs], probe[1, rows, cs]
                    turned[0].append(pltpu.roll(p_re * d_re + p_im * d_im, forth_turn, 1))
                    turned[1].append(pltpu.roll(p_re * d_im - p_im * d_re, forth_turn, 1))
                at = pl.ds(r + half * H + i, step)
                for part in (0, 1):
                    t0, t1 = turned[part]
                    total[part, ct, at, :] += jnp.where(lane >= s, t0, 0.0)
                    total[part, ct + 1, at, :] += jnp.where(lane >= s, t1, t0)
                    total[part, ct + 2, at, :] += jnp.where(lane < s, t1, 0.0)
        return carry

    def visit(p, carry):
        pltpu.make_async_copy(amp_in.at[p], amp.at[p], amp_sems.at[p]).wait()

        @pl.when(alive[p] != 0)
        def _():
            slot(p, 0)

        return carry

    lax.fori_loop(0, SLOTS, visit, 0)
    depth = s_left.shape[1]
    mid = pl.ds(2 * H, W)
    outs = run_copies(
        [
            (total.at[:, :, pl.ds(H + TILE, H)], u_bottom),
            (total.at[:, :, pl.ds(0, H)], u_top),
            (total.at[:, pl.ds(EXT_TILES - depth, depth), mid], s_right),
            (total.at[:, pl.ds(0, depth), mid], s_left),
            (total.at[:, :, pl.ds(H, TILE)], u_mid),
        ],
        out_sems,
    )
    for h in (0, 1):
        for k in range(CHUNKS):
            rows = pl.ds(h * H + 4 * (k // 2), 4)
            cs = pl.ds((k % 2) * LANES, LANES)
            for plane in range(3):
                pack[h, k, pl.ds(4 * plane, 4), :] = grads[plane, rows, cs]
            pack[h, k, pl.ds(12, 4), :] = jnp.zeros((4, LANES), F32)
    outs += run_copies([(pack.at[half], keep), (pack.at[1 - half], give)], sems)
    for copy in outs:
        copy.wait()


ANY = pl.BlockSpec(memory_space=pl.ANY)
HBM = pl.BlockSpec(memory_space=pltpu.HBM)


def sweep(first, corners, alive, objects, probe, amp, tables):
    flops = SLOTS * 24 * 2 * W**3
    depth = 2 if first else 1
    strip = pltpu.HBM((2, depth, W, LANES), F32)
    margin = pltpu.HBM((2, EXT_TILES, H, LANES), F32)
    whole = pltpu.VMEM((2, EXT_TILES, EXT, LANES), F32)
    return pl.pallas_call(
        functools.partial(sweep_kernel, first),
        out_shape=(
            pltpu.HBM((2, EXT_TILES, TILE, LANES), F32),
            jax.ShapeDtypeStruct((2, W, W), F32),
            margin,
            margin,
            strip,
            strip,
            pltpu.HBM((CHUNKS, 16, LANES), F32),
            pltpu.HBM((CHUNKS, 16, LANES), F32),
        ),
        in_specs=[SMEM, SMEM] + [HBM] * len(objects) + [HBM] * (len(probe) + 2),
        out_specs=(HBM, VMEM) + (HBM,) * 6,
        scratch_shapes=[
            whole,
            whole,
            pltpu.VMEM((2, CHUNKS, 16, LANES), F32),
            pltpu.VMEM((SLOTS, W, W), F32),
            pltpu.VMEM((4, 2, W, W), BF16),
            pltpu.VMEM((2, W, W), F32),
            pltpu.VMEM((2, W, W), F32),
            pltpu.VMEM((3, W, W), F32),
            pltpu.VMEM((2 * W, W), BF16),
            pltpu.VMEM((2 * W, W), BF16),
            pltpu.VMEM((2 * W, W), F32),
            pltpu.SemaphoreType.DMA((FIRST_COPIES if first else LATER_COPIES,)),
            pltpu.SemaphoreType.DMA((SLOTS,)),
            pltpu.SemaphoreType.DMA((3,)),
            pltpu.SemaphoreType.DMA((5,)),
            pltpu.VMEM((2, CHUNKS, 8, LANES), F32),
        ],
        compiler_params=pltpu.CompilerParams(vmem_limit_bytes=28 << 20),
        cost_estimate=pl.CostEstimate(flops=flops, bytes_accessed=16 << 20, transcendentals=SLOTS * W * W),
        name="sweep",
    )(corners, alive, *objects, *probe, in_hbm(amp), in_hbm(tables))


ROWS = ((0, H), (H, H + W), (H + W, TILE))


def object_tile(base, total, down, up, weight, mid, edge, put):
    for plane in (0, 1):
        parts = [
            total[plane, 0, 0:H, :] + down[plane, 0],
            total[plane, 0, H : H + W, :],
            total[plane, 0, H + W : TILE, :] + up[plane, 0],
        ]
        if mid is not None:
            parts = [parts[0] + edge[plane, 0, 0:H, :], parts[1] + mid[plane, 0], parts[2] + edge[plane, 0, H:W, :]]
        elif edge is not None:
            parts = [parts[n] + edge[plane, 0, a:b, :] for n, (a, b) in enumerate(ROWS)]
        for n, (a, b) in enumerate(ROWS):
            put(plane, n, base(plane, a, b) + parts[n] * weight[0, a:b, :])


def middle_kernel(tile, left, right, total, down, up, m_left, m_right, e_left, e_right, weight, out, first_rows, last_rows):
    k = pl.program_id(0)

    def put(plane, n, value):
        a, b = ROWS[n]
        out[plane, 0, a:b, :] = value
        if n == 0:
            first_rows[plane, 0] = value
        if n == 2:
            last_rows[plane, 0] = value

    def run(ref, mid, edge):
        object_tile(lambda plane, a, b: ref[plane, a:b, :], total, down, up, weight, mid, edge, put)

    last = EXT_TILES - 1
    pl.when(k == 0)(lambda: run(left, m_left, e_left))
    pl.when(k == 1)(lambda: run(tile, m_left, e_left))
    pl.when((k > 1) & (k < last - 1))(lambda: run(tile, None, None))
    pl.when(k == last - 1)(lambda: run(tile, m_right, e_right))
    pl.when(k == last)(lambda: run(right, m_right, e_right))


def last_kernel(middle, total, down, up, e_left, e_right, weight, out):
    k = pl.program_id(0)

    def put(plane, n, value):
        a, b = ROWS[n]
        out[plane, a:b, :] = value

    def run(edge):
        object_tile(lambda plane, a, b: middle[plane, 0, a:b, :], total, down, up, weight, None, edge, put)

    last = TILE // LANES - 1
    pl.when(k == 0)(lambda: run(e_left))
    pl.when((k > 0) & (k < last))(lambda: run(None))
    pl.when(k == last)(lambda: run(e_right))


def term_specs(offset, depth, last):
    def pick(rows, index):
        return pl.BlockSpec((2, 1, rows, LANES), lambda k: (0, index(k), 0, 0))

    def low(k):
        return jnp.minimum(k, depth - 1)

    def high(k):
        return jnp.maximum(k - last + depth - 1, 0)

    def here(k):
        return k + offset

    strips = [pick(W, low), pick(W, high)] * 2 if depth > 1 else [pick(TILE, low), pick(TILE, high)]
    return [pick(TILE, here), pick(H, here), pick(H, here)] + strips + [
        pl.BlockSpec((1, TILE, LANES), lambda k: (k + offset, 0, 0)),
    ]


def object_step(kernel, grid, in_specs, out_specs, out_shape, name, *args):
    return pl.pallas_call(
        kernel,
        grid=(grid,),
        out_shape=out_shape,
        in_specs=in_specs,
        out_specs=out_specs,
        compiler_params=pltpu.CompilerParams(vmem_limit_bytes=16 << 20),
        cost_estimate=pl.CostEstimate(flops=4 << 20, bytes_accessed=12 << 20, transcendentals=0),
        name=name,
    )(*args)


def middle_step(specimen, left, right, terms, weight):
    tiles = TILE // LANES
    margin = pltpu.HBM((2, EXT_TILES, H, LANES), F32)
    return object_step(
        middle_kernel,
        EXT_TILES,
        [
            pl.BlockSpec((2, TILE, LANES), lambda k: (0, 0, jnp.clip(k - 1, 0, tiles - 1))),
            pl.BlockSpec((2, TILE, LANES), lambda k: (0, 0, 0)),
            pl.BlockSpec((2, TILE, LANES), lambda k: (0, 0, 0)),
        ]
        + term_specs(0, 2, EXT_TILES - 1),
        (pl.BlockSpec((2, 1, TILE, LANES), lambda k: (0, k, 0, 0)),)
        + (pl.BlockSpec((2, 1, H, LANES), lambda k: (0, k, 0, 0)),) * 2,
        (pltpu.HBM((2, EXT_TILES, TILE, LANES), F32), margin, margin),
        "middle",
        in_hbm(specimen),
        left,
        right,
        in_hbm(terms[0]),
        *terms[1:],
        in_hbm(weight),
    )


def last_step(middle, terms, weight):
    tiles = TILE // LANES
    return object_step(
        last_kernel,
        tiles,
        [pl.BlockSpec((2, 1, TILE, LANES), lambda k: (0, k + 1, 0, 0))] + term_specs(1, 1, tiles - 1),
        pl.BlockSpec((2, TILE, LANES), lambda k: (0, 0, k)),
        jax.ShapeDtypeStruct((2, TILE, TILE), F32),
        "last",
        in_hbm(middle),
        in_hbm(terms[0]),
        *terms[1:],
        in_hbm(weight),
    )


PAD_ROWS = TILE + 2 * W
PAD_TILES = (EXT + 2 * W) // LANES


def light_kernel(spots, probe, weight, density, field):
    density[...] = probe[0] * probe[0] + probe[1] * probe[1]
    field[...] = jnp.zeros_like(field)
    step = 16
    lane = lax.broadcasted_iota(jnp.int32, (step, LANES), 1)

    def spot(q, carry):
        r, c, on = spots[3 * q], spots[3 * q + 1], spots[3 * q + 2]

        @pl.when((on != 0) & (r > 0) & (r < W + TILE) & (c > 0) & (c < W + EXT))
        def _():
            ct = jnp.minimum(c // LANES, PAD_TILES - 3)
            s = c - ct * LANES
            turn = lax.rem(s, LANES)
            for i in range(0, W, step):
                at = pl.ds(r + i, step)
                t0 = pltpu.roll(density[pl.ds(i, step), 0:LANES], turn, 1)
                t1 = pltpu.roll(density[pl.ds(i, step), LANES:W], turn, 1)
                field[ct, at, :] += jnp.where(lane >= s, t0, 0.0)
                field[ct + 1, at, :] += jnp.where(lane >= s, t1, t0)
                field[ct + 2, at, :] += jnp.where(lane < s, t1, 0.0)

        return carry

    lax.fori_loop(0, spots.shape[0] // 3, spot, 0)
    for k in range(EXT_TILES):
        weight[k] = 1.0 / (field[W // LANES + k, W : W + TILE, :] + SPECIMEN_REG)


def light(spots, probe):
    return pl.pallas_call(
        light_kernel,
        out_shape=pltpu.HBM((EXT_TILES, TILE, LANES), F32),
        in_specs=[SMEM, VMEM],
        out_specs=VMEM,
        scratch_shapes=[pltpu.VMEM((W, W), F32), pltpu.VMEM((PAD_TILES, PAD_ROWS, LANES), F32)],
        compiler_params=pltpu.CompilerParams(vmem_limit_bytes=12 << 20),
        cost_estimate=pl.CostEstimate(flops=20 << 20, bytes_accessed=20 << 20, transcendentals=0),
        name="light",
    )(spots, probe)


def shift(value, axis, by):
    length = lax.axis_size(axis)
    pairs = [(i, i + by) for i in range(length) if 0 <= i + by < length]
    return lax.ppermute(value, axis, pairs)


def unpack_kernel(half, mine, other, probe, halves):
    halves[half[0]] = mine[...]
    halves[1 - half[0]] = other[...]
    unpack_probe((halves.at[0], halves.at[1]), probe)


def unpack(half, mine, other):
    return pl.pallas_call(
        unpack_kernel,
        out_shape=jax.ShapeDtypeStruct((2, W, W), F32),
        in_specs=[SMEM, VMEM, VMEM],
        out_specs=VMEM,
        scratch_shapes=[pltpu.VMEM((2, CHUNKS, 8, LANES), F32)],
        name="unpack",
    )(half, mine, other)


def sibling(value):
    return lax.ppermute(value, "ty", [(i, i ^ 1) for i in range(lax.axis_size("ty"))])


def in_hbm(value):
    return pltpu.with_memory_space_constraint(value, pltpu.HBM)


def exchange(value):
    rows, columns = lax.axis_size("ty"), lax.axis_size("tx")
    groups = [[i * columns + j for i in range(parity, rows, 2) for j in range(columns)] for parity in (0, 1)]
    return lax.all_to_all(value, BOTH, 0, 0, tiled=True, axis_index_groups=groups)


def probe_step(mine, probe):
    ty, tx = lax.axis_index("ty"), lax.axis_index("tx")
    half, chunk = ty % 2, (ty // 2) * lax.axis_size("tx") + tx
    mine = mine.reshape(CHUNKS, 16, LANES).sum(axis=0)
    start = (0, half * H + 4 * (chunk // 2), LANES * (chunk % 2))
    own = lax.dynamic_slice(probe, start, (2, 4, LANES)).reshape(8, LANES)
    denominator = mine[8:12] + PROBE_REG
    new = own + mine[0:8] / jnp.concatenate([denominator, denominator])
    return jnp.broadcast_to(new, (CHUNKS, 8, LANES)).reshape(CHUNKS * 8, LANES)


def edges(total, down, up, depth, split):
    def strip(lo, hi):
        parts = [total[:, lo:hi, :H] + down[:, lo:hi], total[:, lo:hi, H + W :] + up[:, lo:hi]]
        if not split:
            parts.insert(1, total[:, lo:hi, H : H + W])
        return jnp.concatenate(parts, axis=2)

    return strip(0, depth), strip(EXT_TILES - depth, EXT_TILES)


def finish(swept, probe, weight):
    total, _, u_top, u_bottom, s_left, s_right, keep, give = swept
    depth = s_left.shape[1]
    split = depth > 1
    sums = (keep + sibling(give)).reshape(CHUNKS * 16, LANES)
    down = shift(u_bottom, "ty", 1)
    up = shift(u_top, "ty", -1)
    m_left = shift(s_right, "tx", 1) if split else None
    m_right = shift(s_left, "tx", -1) if split else None
    mine = exchange(sums)
    down, up, m_left, m_right, mine, weight = lax.optimization_barrier((down, up, m_left, m_right, mine, weight))
    low, high = edges(total, down, up, depth, split)
    e_left = shift(high, "tx", 1)
    e_right = shift(low, "tx", -1)
    chunks = exchange(probe_step(mine, probe))
    e_left, e_right, chunks = lax.optimization_barrier((e_left, e_right, chunks))
    chunks = chunks.reshape(CHUNKS, 8, LANES)
    strips = (m_left, m_right, e_left, e_right) if split else (e_left, e_right)
    return (chunks, sibling(chunks)), (total, down, up) + strips, weight


def body(specimen, probe_field, intensity, positions, occupied_slots):
    ty, tx = lax.axis_index("ty"), lax.axis_index("tx")
    row_start = ty * TILE - H
    column_start = tx * TILE - H
    corners = positions - jnp.stack([row_start, column_start])[None, :]
    tables = jnp.asarray(dft_tables())
    half = (ty % 2).reshape(1)
    alive = jnp.concatenate([occupied_slots, half])

    slots = jnp.concatenate([positions, occupied_slots[:, None]], axis=1).astype(F32)
    tag = jnp.pad(slots, ((0, 0), (0, LANES - 3)))
    both = jnp.broadcast_to(tag, (2, SLOTS, LANES))
    left = shift(jnp.concatenate([specimen[:, :, TILE - H :], both], axis=1), "tx", 1)
    right = shift(jnp.concatenate([specimen[:, :, :H], both], axis=1), "tx", -1)
    top = shift(specimen[:, TILE - H :, :], "ty", 1)
    bottom = shift(specimen[:, :H, :], "ty", -1)
    amp = prepare(intensity)
    left, right, top, bottom, amp = lax.optimization_barrier((left, right, top, bottom, amp))
    sides = jnp.stack([left, right], axis=1)
    tags = jnp.stack([sides[0, :, TILE:, :], both])
    corner_top = shift(jnp.concatenate([sides[:, :, TILE - H : TILE, :], tags], axis=2), "ty", 1)
    corner_bottom = shift(jnp.concatenate([sides[:, :, :H, :], tags], axis=2), "ty", -1)

    objects = (in_hbm(specimen), left, right, top, bottom, corner_top, corner_bottom)
    swept = sweep(True, corners, alive, objects, (probe_field,), amp, tables)

    lines = [x[:, :, -SLOTS:, :3].reshape(4, SLOTS, 3)[:3] for x in (corner_top, tags, corner_bottom)]
    around = jnp.concatenate(lines).reshape(9 * SLOTS, 3).astype(jnp.int32)
    spots = (around - jnp.stack([ty * TILE - W, column_start - W, 0])[None, :]).reshape(-1)
    weight = light(spots, probe_field)

    chunks, terms, weight = finish(swept, probe_field, weight)
    middle, first_rows, last_rows = middle_step(specimen, left, right, terms, weight)
    top = shift(last_rows, "ty", 1)
    bottom = shift(first_rows, "ty", -1)

    swept = sweep(False, corners, alive, (in_hbm(middle), top, bottom), chunks, amp, tables)
    probe_field = swept[1]
    weight = light(spots, probe_field)
    chunks, terms, weight = finish(swept, probe_field, weight)
    return last_step(middle, terms, weight), unpack(half, *chunks)


def solution(mesh):
    return jax.shard_map(
        body,
        mesh=mesh,
        in_specs=(
            P(None, "ty", "tx"),
            P(),
            P(BOTH, None, None),
            P(BOTH, None),
            P(BOTH),
        ),
        out_specs=(P(None, "ty", "tx"), P()),
        check_vma=False,
    )
```

```python
import functools
import math

import jax
import jax.numpy as jnp
import numpy as np
from jax import lax
from jax.experimental import pallas as pl
from jax.experimental.pallas import tpu as pltpu
from jax.sharding import PartitionSpec as P

FLOOR = 0.2
SPECIMEN_REG = 0.5
PROBE_REG = 1.0

W = 256
H = W // 2
TILE = 512
EXT = TILE + 2 * H
SLOTS = 8
LANES = 128
EXT_TILES = EXT // LANES
CHUNKS = 64
BOTH = ("ty", "tx")
F32 = jnp.float32
BF16 = jnp.bfloat16
VMEM = pl.BlockSpec(memory_space=pltpu.VMEM)
SMEM = pl.BlockSpec(memory_space=pltpu.SMEM)


def dft_tables():
    j = np.arange(H)[:, None]
    m = np.arange(H)[None, :]
    parts = []
    for odd in (0, 1):
        phase = -2.0 * np.pi * ((m * (2 * j + odd)) % W) / W
        re, im = np.cos(phase) / math.sqrt(W), np.sin(phase) / math.sqrt(W)
        full = np.block([[re, -im], [im, re]])
        for mat in (full, full.T):
            hi = mat.astype(jnp.bfloat16)
            lo = (mat - hi.astype(np.float64)).astype(jnp.bfloat16)
            parts.append(np.stack([hi, lo]))
    return np.stack(parts)


def column_order():
    pick = np.zeros((W, W), np.float32)
    for k in range(H):
        pick[2 * k, k] = 1.0
        pick[2 * k + 1, H + k] = 1.0
    return pick.astype(jnp.bfloat16)


def split2(x):
    hi = x.astype(BF16)
    return hi, (x - hi.astype(F32)).astype(BF16)


def dot(a, b):
    return jnp.dot(a, b, preferred_element_type=F32)


def split3(x):
    hi = x.astype(BF16)
    return (hi,) + split2(x - hi.astype(F32))


def prep_kernel(intensity, pick, pick_t, amp):
    def slot(p, carry):
        hi, mid, lo = split3(jnp.sqrt(intensity[p]))
        x = dot(lo, pick[...]) + dot(mid, pick[...]) + dot(hi, pick[...])
        hi, mid, lo = split3(x)
        amp[p] = dot(pick_t[...], lo) + dot(pick_t[...], mid) + dot(pick_t[...], hi)
        return carry

    lax.fori_loop(0, SLOTS, slot, 0)


def prepare(intensity):
    pick = column_order()
    return pl.pallas_call(
        prep_kernel,
        out_shape=pltpu.HBM((SLOTS, W, W), F32),
        in_specs=[VMEM, VMEM, VMEM],
        out_specs=VMEM,
        cost_estimate=pl.CostEstimate(flops=4 * 3 * SLOTS * W**3, bytes_accessed=16 * SLOTS * W * W, transcendentals=SLOTS * W * W),
        name="amplitudes",
    )(intensity, jnp.asarray(pick), jnp.asarray(pick.T))


def run_copies(pairs, sems):
    copies = [pltpu.make_async_copy(src, dst, sems.at[n]) for n, (src, dst) in enumerate(pairs)]
    for copy in copies:
        copy.start()
    return copies


def first_loads(refs, ext):
    tile, left, right, top, bottom, corner_top, corner_bottom = refs
    inner, upper, lower = pl.ds(H, TILE), pl.ds(0, H), pl.ds(H + TILE, H)
    last = EXT_TILES - 1
    pairs = [
        (left.at[:, pl.ds(0, TILE)], ext.at[:, 0, inner]),
        (right.at[:, pl.ds(0, TILE)], ext.at[:, last, inner]),
        (corner_top.at[:, 0, pl.ds(0, H)], ext.at[:, 0, upper]),
        (corner_top.at[:, 1, pl.ds(0, H)], ext.at[:, last, upper]),
        (corner_bottom.at[:, 0, pl.ds(0, H)], ext.at[:, 0, lower]),
        (corner_bottom.at[:, 1, pl.ds(0, H)], ext.at[:, last, lower]),
    ]
    for k in range(TILE // LANES):
        cs = pl.ds(k * LANES, LANES)
        pairs.append((tile.at[:, :, cs], ext.at[:, 1 + k, inner]))
        pairs.append((top.at[:, :, cs], ext.at[:, 1 + k, upper]))
        pairs.append((bottom.at[:, :, cs], ext.at[:, 1 + k, lower]))
    return pairs


def later_loads(refs, ext):
    middle, top, bottom = refs
    return [
        (middle, ext.at[:, :, pl.ds(H, TILE)]),
        (top, ext.at[:, :, pl.ds(0, H)]),
        (bottom, ext.at[:, :, pl.ds(H + TILE, H)]),
    ]


FIRST_COPIES = 18
LATER_COPIES = 3


def unpack_probe(halves, probe):
    for h, chunks in enumerate(halves):
        for k in range(CHUNKS):
            rows = pl.ds(h * H + 4 * (k // 2), 4)
            cs = pl.ds((k % 2) * LANES, LANES)
            probe[0, rows, cs] = chunks[k, 0:4, :]
            probe[1, rows, cs] = chunks[k, 4:8, :]


def sweep_kernel(first, corners, alive, *refs):
    n, m = (7, 1) if first else (3, 2)
    objects, probe_in, (amp_in, tables_in) = refs[:n], refs[n : n + m], refs[n + m : n + m + 2]
    rest = refs[n + m + 2 :]
    half = alive[SLOTS]
    u_mid, probe, u_top, u_bottom, s_left, s_right, keep, give = rest[:8]
    total, ext, pack, amp, tables, windows, exit_waves, grads, his, los, wides, ext_sems, amp_sems, sems, out_sems, halves = rest[8:]
    loads = first_loads if first else later_loads
    copies = run_copies(loads(objects, ext), ext_sems)
    more = [(tables_in, tables)]
    if first:
        more.append((probe_in[0], probe))
    else:
        more += [(probe_in[0], halves.at[half]), (probe_in[1], halves.at[1 - half])]
    copies += run_copies(more, sems)
    run_copies([(amp_in.at[p], amp.at[p]) for p in range(SLOTS)], amp_sems)
    total[...] = jnp.zeros_like(total)
    grads[...] = jnp.zeros_like(grads)
    even, even_t, odd, odd_t = 0, 1, 2, 3
    step = 16
    lane = lax.broadcasted_iota(jnp.int32, (step, LANES), 1)
    for copy in copies:
        copy.wait()
    if not first:
        unpack_probe((halves.at[0], halves.at[1]), probe)

    def slot(p, z):
        window, exit_wave = windows.at[z], exit_waves.at[z]
        a_hi, a_lo, wide = his.at[z], los.at[z], wides.at[z]

        def left_dot(t, branch):
            rows = pl.ds(branch * W, W)
            hi, lo = a_hi[rows, :], a_lo[rows, :]
            wide[rows, :] = dot(tables[t, 0], hi) + dot(tables[t, 1], hi) + dot(tables[t, 0], lo)

        def right_dot(t, branch):
            rows = pl.ds(branch * W, W)
            hi, lo = a_hi[rows, :], a_lo[rows, :]
            wide[rows, :] = dot(hi, tables[t, 0]) + dot(hi, tables[t, 1]) + dot(lo, tables[t, 0])

        def put(row, col, value):
            hi, lo = split2(value)
            a_hi[pl.ds(row, step), pl.ds(col, LANES)] = hi
            a_lo[pl.ds(row, step), pl.ds(col, LANES)] = lo

        live = alive[p].astype(F32)
        r = corners[p, 0]
        c = corners[p, 1]
        ct = jnp.minimum(c // LANES, EXT_TILES - 3)
        s = c - ct * LANES
        back_turn = lax.rem(LANES - s, LANES)
        forth_turn = lax.rem(s, LANES)

        for i in range(0, H, step):
            waves = []
            for half in (0, 1):
                parts = []
                for plane in (0, 1):
                    turned = [
                        pltpu.roll(ext[plane, ct + k, pl.ds(r + half * H + i, step), :], back_turn, 1)
                        for k in range(3)
                    ]
                    cols = [jnp.where(lane < LANES - s, turned[k], turned[k + 1]) for k in (0, 1)]
                    parts.append(cols)
                rows = pl.ds(half * H + i, step)
                wave = []
                for k in (0, 1):
                    cs = pl.ds(k * LANES, LANES)
                    o_re, o_im = parts[0][k], parts[1][k]
                    p_re, p_im = probe[0, rows, cs], probe[1, rows, cs]
                    w_re = p_re * o_re - p_im * o_im
                    w_im = p_re * o_im + p_im * o_re
                    window[0, rows, cs] = o_re
                    window[1, rows, cs] = o_im
                    exit_wave[0, rows, cs] = w_re
                    exit_wave[1, rows, cs] = w_im
                    wave.append((w_re, w_im))
                waves.append(wave)
            for k in (0, 1):
                for part in (0, 1):
                    x0, x1 = waves[0][k][part], waves[1][k][part]
                    put(part * H + i, k * LANES, x0 + x1)
                    put(W + part * H + i, k * LANES, x0 - x1)
        left_dot(even, 0)
        left_dot(odd, 1)
        yield

        for branch in (0, 1):
            for i in range(0, H, step):
                for part in (0, 1):
                    rows = pl.ds(branch * W + part * H + i, step)
                    x0, x1 = wide[rows, 0:LANES], wide[rows, LANES:W]
                    put(branch * H + i, part * LANES, x0 + x1)
                    put(W + branch * H + i, part * LANES, x0 - x1)
        right_dot(even_t, 0)
        right_dot(odd_t, 1)
        yield

        for branch in (0, 1):
            for i in range(0, W, step):
                rows = pl.ds(branch * W + i, step)
                z_re, z_im = wide[rows, 0:LANES], wide[rows, LANES:W]
                power = z_re * z_re + z_im * z_im
                factor = amp[p, pl.ds(i, step), pl.ds(branch * LANES, LANES)] * lax.rsqrt(
                    jnp.maximum(power, FLOOR * FLOOR)
                )
                put(branch * W + i, 0, z_re * factor)
                put(branch * W + i, LANES, z_im * factor)
        right_dot(even, 0)
        right_dot(odd, 1)
        yield

        for branch in (0, 1):
            for i in range(0, H, step):
                rows_e = pl.ds(branch * H + i, step)
                rows_o = pl.ds(W + branch * H + i, step)
                for part in (0, 1):
                    cs = pl.ds(part * LANES, LANES)
                    x0, x1 = wide[rows_e, cs], wide[rows_o, cs]
                    put(branch * W + part * H + i, 0, x0 + x1)
                    put(branch * W + part * H + i, LANES, x0 - x1)
        left_dot(even_t, 0)
        left_dot(odd_t, 1)
        yield

        for i in range(0, H, step):
            for half in (0, 1):
                rows = pl.ds(half * H + i, step)
                turned = [[], []]
                for k in (0, 1):
                    cs = pl.ds(k * LANES, LANES)
                    back = []
                    for part in (0, 1):
                        x0 = wide[pl.ds(part * H + i, step), cs]
                        x1 = wide[pl.ds(W + part * H + i, step), cs]
                        back.append(x0 + x1 if half == 0 else x0 - x1)
                    d_re = live * (back[0] - exit_wave[0, rows, cs])
                    d_im = live * (back[1] - exit_wave[1, rows, cs])
                    o_re, o_im = window[0, rows, cs], window[1, rows, cs]
                    grads[0, rows, cs] += o_re * d_re + o_im * d_im
                    grads[1, rows, cs] += o_re * d_im - o_im * d_re
                    grads[2, rows, cs] += live * (o_re * o_re + o_im * o_im)
                    p_re, p_im = probe[0, rows, cs], probe[1, rows, cs]
                    turned[0].append(pltpu.roll(p_re * d_re + p_im * d_im, forth_turn, 1))
                    turned[1].append(pltpu.roll(p_re * d_im - p_im * d_re, forth_turn, 1))
                at = pl.ds(r + half * H + i, step)
                for part in (0, 1):
                    t0, t1 = turned[part]
                    total[part, ct, at, :] += jnp.where(lane >= s, t0, 0.0)
                    total[part, ct + 1, at, :] += jnp.where(lane >= s, t1, t0)
                    total[part, ct + 2, at, :] += jnp.where(lane < s, t1, 0.0)

    def pair(q, carry):
        for z in (0, 1):
            pltpu.make_async_copy(amp_in.at[2 * q + z], amp.at[2 * q + z], amp_sems.at[2 * q + z]).wait()

        @pl.when((alive[2 * q] != 0) | (alive[2 * q + 1] != 0))
        def _():
            runs = [slot(2 * q, 0), slot(2 * q + 1, 1)]
            for _ in range(5):
                for run in runs:
                    next(run, None)

        return carry

    lax.fori_loop(0, SLOTS // 2, pair, 0)
    depth = s_left.shape[1]
    mid = pl.ds(2 * H, W)
    outs = run_copies(
        [
            (total.at[:, :, pl.ds(H + TILE, H)], u_bottom),
            (total.at[:, :, pl.ds(0, H)], u_top),
            (total.at[:, pl.ds(EXT_TILES - depth, depth), mid], s_right),
            (total.at[:, pl.ds(0, depth), mid], s_left),
            (total.at[:, :, pl.ds(H, TILE)], u_mid),
        ],
        out_sems,
    )
    for h in (0, 1):
        for k in range(CHUNKS):
            rows = pl.ds(h * H + 4 * (k // 2), 4)
            cs = pl.ds((k % 2) * LANES, LANES)
            for plane in range(3):
                pack[h, k, pl.ds(4 * plane, 4), :] = grads[plane, rows, cs]
            pack[h, k, pl.ds(12, 4), :] = jnp.zeros((4, LANES), F32)
    outs += run_copies([(pack.at[half], keep), (pack.at[1 - half], give)], sems)
    for copy in outs:
        copy.wait()


ANY = pl.BlockSpec(memory_space=pl.ANY)
HBM = pl.BlockSpec(memory_space=pltpu.HBM)


def sweep(first, corners, alive, objects, probe, amp, tables):
    flops = SLOTS * 24 * 2 * W**3
    depth = 2 if first else 1
    strip = pltpu.HBM((2, depth, W, LANES), F32)
    margin = pltpu.HBM((2, EXT_TILES, H, LANES), F32)
    whole = pltpu.VMEM((2, EXT_TILES, EXT, LANES), F32)
    return pl.pallas_call(
        functools.partial(sweep_kernel, first),
        out_shape=(
            pltpu.HBM((2, EXT_TILES, TILE, LANES), F32),
            jax.ShapeDtypeStruct((2, W, W), F32),
            margin,
            margin,
            strip,
            strip,
            pltpu.HBM((CHUNKS, 16, LANES), F32),
            pltpu.HBM((CHUNKS, 16, LANES), F32),
        ),
        in_specs=[SMEM, SMEM] + [HBM] * len(objects) + [HBM] * (len(probe) + 2),
        out_specs=(HBM, VMEM) + (HBM,) * 6,
        scratch_shapes=[
            whole,
            whole,
            pltpu.VMEM((2, CHUNKS, 16, LANES), F32),
            pltpu.VMEM((SLOTS, W, W), F32),
            pltpu.VMEM((4, 2, W, W), BF16),
            pltpu.VMEM((2, 2, W, W), F32),
            pltpu.VMEM((2, 2, W, W), F32),
            pltpu.VMEM((3, W, W), F32),
            pltpu.VMEM((2, 2 * W, W), BF16),
            pltpu.VMEM((2, 2 * W, W), BF16),
            pltpu.VMEM((2, 2 * W, W), F32),
            pltpu.SemaphoreType.DMA((FIRST_COPIES if first else LATER_COPIES,)),
            pltpu.SemaphoreType.DMA((SLOTS,)),
            pltpu.SemaphoreType.DMA((3,)),
            pltpu.SemaphoreType.DMA((5,)),
            pltpu.VMEM((2, CHUNKS, 8, LANES), F32),
        ],
        compiler_params=pltpu.CompilerParams(vmem_limit_bytes=28 << 20),
        cost_estimate=pl.CostEstimate(flops=flops, bytes_accessed=16 << 20, transcendentals=SLOTS * W * W),
        name="sweep",
    )(corners, alive, *objects, *probe, in_hbm(amp), in_hbm(tables))


ROWS = ((0, H), (H, H + W), (H + W, TILE))


def object_tile(base, total, down, up, weight, mid, edge, put):
    for plane in (0, 1):
        parts = [
            total[plane, 0, 0:H, :] + down[plane, 0],
            total[plane, 0, H : H + W, :],
            total[plane, 0, H + W : TILE, :] + up[plane, 0],
        ]
        if mid is not None:
            parts = [parts[0] + edge[plane, 0, 0:H, :], parts[1] + mid[plane, 0], parts[2] + edge[plane, 0, H:W, :]]
        elif edge is not None:
            parts = [parts[n] + edge[plane, 0, a:b, :] for n, (a, b) in enumerate(ROWS)]
        for n, (a, b) in enumerate(ROWS):
            put(plane, n, base(plane, a, b) + parts[n] * weight[0, a:b, :])


def middle_kernel(tile, left, right, total, down, up, m_left, m_right, e_left, e_right, weight, out, first_rows, last_rows):
    k = pl.program_id(0)

    def put(plane, n, value):
        a, b = ROWS[n]
        out[plane, 0, a:b, :] = value
        if n == 0:
            first_rows[plane, 0] = value
        if n == 2:
            last_rows[plane, 0] = value

    def run(ref, mid, edge):
        object_tile(lambda plane, a, b: ref[plane, a:b, :], total, down, up, weight, mid, edge, put)

    last = EXT_TILES - 1
    pl.when(k == 0)(lambda: run(left, m_left, e_left))
    pl.when(k == 1)(lambda: run(tile, m_left, e_left))
    pl.when((k > 1) & (k < last - 1))(lambda: run(tile, None, None))
    pl.when(k == last - 1)(lambda: run(tile, m_right, e_right))
    pl.when(k == last)(lambda: run(right, m_right, e_right))


def last_kernel(middle, total, down, up, e_left, e_right, weight, out):
    k = pl.program_id(0)

    def put(plane, n, value):
        a, b = ROWS[n]
        out[plane, a:b, :] = value

    def run(edge):
        object_tile(lambda plane, a, b: middle[plane, 0, a:b, :], total, down, up, weight, None, edge, put)

    last = TILE // LANES - 1
    pl.when(k == 0)(lambda: run(e_left))
    pl.when((k > 0) & (k < last))(lambda: run(None))
    pl.when(k == last)(lambda: run(e_right))


def term_specs(offset, depth, last):
    def pick(rows, index):
        return pl.BlockSpec((2, 1, rows, LANES), lambda k: (0, index(k), 0, 0))

    def low(k):
        return jnp.minimum(k, depth - 1)

    def high(k):
        return jnp.maximum(k - last + depth - 1, 0)

    def here(k):
        return k + offset

    strips = [pick(W, low), pick(W, high)] * 2 if depth > 1 else [pick(TILE, low), pick(TILE, high)]
    return [pick(TILE, here), pick(H, here), pick(H, here)] + strips + [
        pl.BlockSpec((1, TILE, LANES), lambda k: (k + offset, 0, 0)),
    ]


def object_step(kernel, grid, in_specs, out_specs, out_shape, name, *args):
    return pl.pallas_call(
        kernel,
        grid=(grid,),
        out_shape=out_shape,
        in_specs=in_specs,
        out_specs=out_specs,
        compiler_params=pltpu.CompilerParams(vmem_limit_bytes=16 << 20),
        cost_estimate=pl.CostEstimate(flops=4 << 20, bytes_accessed=12 << 20, transcendentals=0),
        name=name,
    )(*args)


def middle_step(specimen, left, right, terms, weight):
    tiles = TILE // LANES
    margin = pltpu.HBM((2, EXT_TILES, H, LANES), F32)
    return object_step(
        middle_kernel,
        EXT_TILES,
        [
            pl.BlockSpec((2, TILE, LANES), lambda k: (0, 0, jnp.clip(k - 1, 0, tiles - 1))),
            pl.BlockSpec((2, TILE, LANES), lambda k: (0, 0, 0)),
            pl.BlockSpec((2, TILE, LANES), lambda k: (0, 0, 0)),
        ]
        + term_specs(0, 2, EXT_TILES - 1),
        (pl.BlockSpec((2, 1, TILE, LANES), lambda k: (0, k, 0, 0)),)
        + (pl.BlockSpec((2, 1, H, LANES), lambda k: (0, k, 0, 0)),) * 2,
        (pltpu.HBM((2, EXT_TILES, TILE, LANES), F32), margin, margin),
        "middle",
        in_hbm(specimen),
        left,
        right,
        in_hbm(terms[0]),
        *terms[1:],
        in_hbm(weight),
    )


def last_step(middle, terms, weight):
    tiles = TILE // LANES
    return object_step(
        last_kernel,
        tiles,
        [pl.BlockSpec((2, 1, TILE, LANES), lambda k: (0, k + 1, 0, 0))] + term_specs(1, 1, tiles - 1),
        pl.BlockSpec((2, TILE, LANES), lambda k: (0, 0, k)),
        jax.ShapeDtypeStruct((2, TILE, TILE), F32),
        "last",
        in_hbm(middle),
        in_hbm(terms[0]),
        *terms[1:],
        in_hbm(weight),
    )


PAD_ROWS = TILE + 2 * W
PAD_TILES = (EXT + 2 * W) // LANES


def light_kernel(spots, probe, weight, density, field):
    density[...] = probe[0] * probe[0] + probe[1] * probe[1]
    field[...] = jnp.zeros_like(field)
    step = 16
    lane = lax.broadcasted_iota(jnp.int32, (step, LANES), 1)

    def spot(q, carry):
        r, c, on = spots[3 * q], spots[3 * q + 1], spots[3 * q + 2]

        @pl.when((on != 0) & (r > 0) & (r < W + TILE) & (c > 0) & (c < W + EXT))
        def _():
            ct = jnp.minimum(c // LANES, PAD_TILES - 3)
            s = c - ct * LANES
            turn = lax.rem(s, LANES)
            for i in range(0, W, step):
                at = pl.ds(r + i, step)
                t0 = pltpu.roll(density[pl.ds(i, step), 0:LANES], turn, 1)
                t1 = pltpu.roll(density[pl.ds(i, step), LANES:W], turn, 1)
                field[ct, at, :] += jnp.where(lane >= s, t0, 0.0)
                field[ct + 1, at, :] += jnp.where(lane >= s, t1, t0)
                field[ct + 2, at, :] += jnp.where(lane < s, t1, 0.0)

        return carry

    lax.fori_loop(0, spots.shape[0] // 3, spot, 0)
    for k in range(EXT_TILES):
        weight[k] = 1.0 / (field[W // LANES + k, W : W + TILE, :] + SPECIMEN_REG)


def light(spots, probe):
    return pl.pallas_call(
        light_kernel,
        out_shape=pltpu.HBM((EXT_TILES, TILE, LANES), F32),
        in_specs=[SMEM, VMEM],
        out_specs=VMEM,
        scratch_shapes=[pltpu.VMEM((W, W), F32), pltpu.VMEM((PAD_TILES, PAD_ROWS, LANES), F32)],
        compiler_params=pltpu.CompilerParams(vmem_limit_bytes=12 << 20),
        cost_estimate=pl.CostEstimate(flops=20 << 20, bytes_accessed=20 << 20, transcendentals=0),
        name="light",
    )(spots, probe)


def shift(value, axis, by):
    length = lax.axis_size(axis)
    pairs = [(i, i + by) for i in range(length) if 0 <= i + by < length]
    return lax.ppermute(value, axis, pairs)


def unpack_kernel(half, mine, other, probe, halves):
    halves[half[0]] = mine[...]
    halves[1 - half[0]] = other[...]
    unpack_probe((halves.at[0], halves.at[1]), probe)


def unpack(half, mine, other):
    return pl.pallas_call(
        unpack_kernel,
        out_shape=jax.ShapeDtypeStruct((2, W, W), F32),
        in_specs=[SMEM, VMEM, VMEM],
        out_specs=VMEM,
        scratch_shapes=[pltpu.VMEM((2, CHUNKS, 8, LANES), F32)],
        name="unpack",
    )(half, mine, other)


def sibling(value):
    return lax.ppermute(value, "ty", [(i, i ^ 1) for i in range(lax.axis_size("ty"))])


def in_hbm(value):
    return pltpu.with_memory_space_constraint(value, pltpu.HBM)


def exchange(value):
    rows, columns = lax.axis_size("ty"), lax.axis_size("tx")
    groups = [[i * columns + j for i in range(parity, rows, 2) for j in range(columns)] for parity in (0, 1)]
    return lax.all_to_all(value, BOTH, 0, 0, tiled=True, axis_index_groups=groups)


def probe_step(mine, probe):
    ty, tx = lax.axis_index("ty"), lax.axis_index("tx")
    half, chunk = ty % 2, (ty // 2) * lax.axis_size("tx") + tx
    mine = mine.reshape(CHUNKS, 16, LANES).sum(axis=0)
    start = (0, half * H + 4 * (chunk // 2), LANES * (chunk % 2))
    own = lax.dynamic_slice(probe, start, (2, 4, LANES)).reshape(8, LANES)
    denominator = mine[8:12] + PROBE_REG
    new = own + mine[0:8] / jnp.concatenate([denominator, denominator])
    return jnp.broadcast_to(new, (CHUNKS, 8, LANES)).reshape(CHUNKS * 8, LANES)


def edges(total, down, up, depth, split):
    def strip(lo, hi):
        parts = [total[:, lo:hi, :H] + down[:, lo:hi], total[:, lo:hi, H + W :] + up[:, lo:hi]]
        if not split:
            parts.insert(1, total[:, lo:hi, H : H + W])
        return jnp.concatenate(parts, axis=2)

    return strip(0, depth), strip(EXT_TILES - depth, EXT_TILES)


def finish(swept, probe, weight):
    total, _, u_top, u_bottom, s_left, s_right, keep, give = swept
    depth = s_left.shape[1]
    split = depth > 1
    sums = (keep + sibling(give)).reshape(CHUNKS * 16, LANES)
    down = shift(u_bottom, "ty", 1)
    up = shift(u_top, "ty", -1)
    m_left = shift(s_right, "tx", 1) if split else None
    m_right = shift(s_left, "tx", -1) if split else None
    mine = exchange(sums)
    down, up, m_left, m_right, mine, weight = lax.optimization_barrier((down, up, m_left, m_right, mine, weight))
    low, high = edges(total, down, up, depth, split)
    e_left = shift(high, "tx", 1)
    e_right = shift(low, "tx", -1)
    chunks = exchange(probe_step(mine, probe))
    e_left, e_right, chunks = lax.optimization_barrier((e_left, e_right, chunks))
    chunks = chunks.reshape(CHUNKS, 8, LANES)
    strips = (m_left, m_right, e_left, e_right) if split else (e_left, e_right)
    return (chunks, sibling(chunks)), (total, down, up) + strips, weight


def body(specimen, probe_field, intensity, positions, occupied_slots):
    ty, tx = lax.axis_index("ty"), lax.axis_index("tx")
    row_start = ty * TILE - H
    column_start = tx * TILE - H
    corners = positions - jnp.stack([row_start, column_start])[None, :]
    tables = jnp.asarray(dft_tables())
    half = (ty % 2).reshape(1)
    alive = jnp.concatenate([occupied_slots, half])

    slots = jnp.concatenate([positions, occupied_slots[:, None]], axis=1).astype(F32)
    tag = jnp.pad(slots, ((0, 0), (0, LANES - 3)))
    both = jnp.broadcast_to(tag, (2, SLOTS, LANES))
    left = shift(jnp.concatenate([specimen[:, :, TILE - H :], both], axis=1), "tx", 1)
    right = shift(jnp.concatenate([specimen[:, :, :H], both], axis=1), "tx", -1)
    top = shift(specimen[:, TILE - H :, :], "ty", 1)
    bottom = shift(specimen[:, :H, :], "ty", -1)
    amp = prepare(intensity)
    left, right, top, bottom, amp = lax.optimization_barrier((left, right, top, bottom, amp))
    sides = jnp.stack([left, right], axis=1)
    tags = jnp.stack([sides[0, :, TILE:, :], both])
    corner_top = shift(jnp.concatenate([sides[:, :, TILE - H : TILE, :], tags], axis=2), "ty", 1)
    corner_bottom = shift(jnp.concatenate([sides[:, :, :H, :], tags], axis=2), "ty", -1)

    objects = (in_hbm(specimen), left, right, top, bottom, corner_top, corner_bottom)
    swept = sweep(True, corners, alive, objects, (probe_field,), amp, tables)

    lines = [x[:, :, -SLOTS:, :3].reshape(4, SLOTS, 3)[:3] for x in (corner_top, tags, corner_bottom)]
    around = jnp.concatenate(lines).reshape(9 * SLOTS, 3).astype(jnp.int32)
    spots = (around - jnp.stack([ty * TILE - W, column_start - W, 0])[None, :]).reshape(-1)
    weight = light(spots, probe_field)

    chunks, terms, weight = finish(swept, probe_field, weight)
    middle, first_rows, last_rows = middle_step(specimen, left, right, terms, weight)
    top = shift(last_rows, "ty", 1)
    bottom = shift(first_rows, "ty", -1)

    swept = sweep(False, corners, alive, (in_hbm(middle), top, bottom), chunks, amp, tables)
    probe_field = swept[1]
    weight = light(spots, probe_field)
    chunks, terms, weight = finish(swept, probe_field, weight)
    return last_step(middle, terms, weight), unpack(half, *chunks)


def solution(mesh):
    return jax.shard_map(
        body,
        mesh=mesh,
        in_specs=(
            P(None, "ty", "tx"),
            P(),
            P(BOTH, None, None),
            P(BOTH, None),
            P(BOTH),
        ),
        out_specs=(P(None, "ty", "tx"), P()),
        check_vma=False,
    )
```

```python
import functools
import math

import jax
import jax.numpy as jnp
import numpy as np
from jax import lax
from jax.experimental import pallas as pl
from jax.experimental.pallas import tpu as pltpu
from jax.sharding import PartitionSpec as P

FLOOR = 0.2
SPECIMEN_REG = 0.5
PROBE_REG = 1.0

W = 256
H = W // 2
TILE = 512
EXT = TILE + 2 * H
SLOTS = 8
LANES = 128
EXT_TILES = EXT // LANES
CHUNKS = 64
BOTH = ("ty", "tx")
F32 = jnp.float32
BF16 = jnp.bfloat16
VMEM = pl.BlockSpec(memory_space=pltpu.VMEM)
SMEM = pl.BlockSpec(memory_space=pltpu.SMEM)


def dft_tables():
    j = np.arange(H)[:, None]
    m = np.arange(H)[None, :]
    parts = []
    for odd in (0, 1):
        phase = -2.0 * np.pi * ((m * (2 * j + odd)) % W) / W
        re, im = np.cos(phase) / math.sqrt(W), np.sin(phase) / math.sqrt(W)
        full = np.block([[re, -im], [im, re]])
        for mat in (full, full.T):
            hi = mat.astype(jnp.bfloat16)
            lo = (mat - hi.astype(np.float64)).astype(jnp.bfloat16)
            parts.append(np.stack([hi, lo]))
    return np.stack(parts)


def column_order():
    pick = np.zeros((W, W), np.float32)
    for k in range(H):
        pick[2 * k, k] = 1.0
        pick[2 * k + 1, H + k] = 1.0
    return pick.astype(jnp.bfloat16)


def split2(x):
    hi = x.astype(BF16)
    return hi, (x - hi.astype(F32)).astype(BF16)


def dot(a, b):
    return jnp.dot(a, b, preferred_element_type=F32)


def split3(x):
    hi = x.astype(BF16)
    return (hi,) + split2(x - hi.astype(F32))


def prep_kernel(intensity, pick, pick_t, amp):
    def slot(p, carry):
        hi, mid, lo = split3(jnp.sqrt(intensity[p]))
        x = dot(lo, pick[...]) + dot(mid, pick[...]) + dot(hi, pick[...])
        hi, mid, lo = split3(x)
        amp[p] = dot(pick_t[...], lo) + dot(pick_t[...], mid) + dot(pick_t[...], hi)
        return carry

    lax.fori_loop(0, SLOTS, slot, 0)


def prepare(intensity):
    pick = column_order()
    return pl.pallas_call(
        prep_kernel,
        out_shape=pltpu.HBM((SLOTS, W, W), F32),
        in_specs=[VMEM, VMEM, VMEM],
        out_specs=VMEM,
        cost_estimate=pl.CostEstimate(flops=4 * 3 * SLOTS * W**3, bytes_accessed=16 * SLOTS * W * W, transcendentals=SLOTS * W * W),
        name="amplitudes",
    )(intensity, jnp.asarray(pick), jnp.asarray(pick.T))


def run_copies(pairs, sems):
    copies = [pltpu.make_async_copy(src, dst, sems.at[n]) for n, (src, dst) in enumerate(pairs)]
    for copy in copies:
        copy.start()
    return copies


def first_loads(refs, ext):
    tile, left, right, top, bottom, corner_top, corner_bottom = refs
    inner, upper, lower = pl.ds(H, TILE), pl.ds(0, H), pl.ds(H + TILE, H)
    last = EXT_TILES - 1
    pairs = [
        (left.at[:, pl.ds(0, TILE)], ext.at[:, 0, inner]),
        (right.at[:, pl.ds(0, TILE)], ext.at[:, last, inner]),
        (corner_top.at[:, 0, pl.ds(0, H)], ext.at[:, 0, upper]),
        (corner_top.at[:, 1, pl.ds(0, H)], ext.at[:, last, upper]),
        (corner_bottom.at[:, 0, pl.ds(0, H)], ext.at[:, 0, lower]),
        (corner_bottom.at[:, 1, pl.ds(0, H)], ext.at[:, last, lower]),
    ]
    for k in range(TILE // LANES):
        cs = pl.ds(k * LANES, LANES)
        pairs.append((tile.at[:, :, cs], ext.at[:, 1 + k, inner]))
        pairs.append((top.at[:, :, cs], ext.at[:, 1 + k, upper]))
        pairs.append((bottom.at[:, :, cs], ext.at[:, 1 + k, lower]))
    return pairs


def later_loads(refs, ext):
    *rows, top, bottom = refs
    return [(x, ext.at[:, :, pl.ds(H * (n + 1), H)]) for n, x in enumerate(rows)] + [
        (top, ext.at[:, :, pl.ds(0, H)]),
        (bottom, ext.at[:, :, pl.ds(H + TILE, H)]),
    ]


FIRST_COPIES = 18
LATER_COPIES = 6


def unpack_probe(halves, probe):
    for h, chunks in enumerate(halves):
        for k in range(CHUNKS):
            rows = pl.ds(h * H + 4 * (k // 2), 4)
            cs = pl.ds((k % 2) * LANES, LANES)
            probe[0, rows, cs] = chunks[k, 0:4, :]
            probe[1, rows, cs] = chunks[k, 4:8, :]


def sweep_kernel(first, corners, alive, *refs):
    n, m = (7, 1) if first else (6, 2)
    objects, probe_in, (amp_in, tables_in) = refs[:n], refs[n : n + m], refs[n + m : n + m + 2]
    rest = refs[n + m + 2 :]
    half = alive[SLOTS]
    u_mid, probe, u_top, u_bottom, s_left, s_right, keep, give = rest[:8]
    total, ext, pack, amp, tables, windows, exit_waves, grads, his, los, wides, ext_sems, amp_sems, sems, out_sems, halves = rest[8:]
    loads = first_loads if first else later_loads
    copies = run_copies(loads(objects, ext), ext_sems)
    more = [(tables_in, tables)]
    if first:
        more.append((probe_in[0], probe))
    else:
        more += [(probe_in[0], halves.at[half]), (probe_in[1], halves.at[1 - half])]
    copies += run_copies(more, sems)
    run_copies([(amp_in.at[p], amp.at[p]) for p in range(SLOTS)], amp_sems)
    total[...] = jnp.zeros_like(total)
    grads[...] = jnp.zeros_like(grads)
    even, even_t, odd, odd_t = 0, 1, 2, 3
    step = 16
    lane = lax.broadcasted_iota(jnp.int32, (step, LANES), 1)
    for copy in copies:
        copy.wait()
    if not first:
        unpack_probe((halves.at[0], halves.at[1]), probe)

    def slot(p, z):
        window, exit_wave = windows.at[z], exit_waves.at[z]
        a_hi, a_lo, wide = his.at[z], los.at[z], wides.at[z]

        def left_dot(t, branch):
            rows = pl.ds(branch * W, W)
            hi, lo = a_hi[rows, :], a_lo[rows, :]
            wide[rows, :] = dot(tables[t, 0], hi) + dot(tables[t, 1], hi) + dot(tables[t, 0], lo)

        def right_dot(t, branch):
            rows = pl.ds(branch * W, W)
            hi, lo = a_hi[rows, :], a_lo[rows, :]
            wide[rows, :] = dot(hi, tables[t, 0]) + dot(hi, tables[t, 1]) + dot(lo, tables[t, 0])

        def put(row, col, value):
            hi, lo = split2(value)
            a_hi[pl.ds(row, step), pl.ds(col, LANES)] = hi
            a_lo[pl.ds(row, step), pl.ds(col, LANES)] = lo

        live = alive[p].astype(F32)
        r = corners[p, 0]
        c = corners[p, 1]
        ct = jnp.minimum(c // LANES, EXT_TILES - 3)
        s = c - ct * LANES
        back_turn = lax.rem(LANES - s, LANES)
        forth_turn = lax.rem(s, LANES)

        for i in range(0, H, step):
            waves = []
            for half in (0, 1):
                parts = []
                for plane in (0, 1):
                    turned = [
                        pltpu.roll(ext[plane, ct + k, pl.ds(r + half * H + i, step), :], back_turn, 1)
                        for k in range(3)
                    ]
                    cols = [jnp.where(lane < LANES - s, turned[k], turned[k + 1]) for k in (0, 1)]
                    parts.append(cols)
                rows = pl.ds(half * H + i, step)
                wave = []
                for k in (0, 1):
                    cs = pl.ds(k * LANES, LANES)
                    o_re, o_im = parts[0][k], parts[1][k]
                    p_re, p_im = probe[0, rows, cs], probe[1, rows, cs]
                    w_re = p_re * o_re - p_im * o_im
                    w_im = p_re * o_im + p_im * o_re
                    window[0, rows, cs] = o_re
                    window[1, rows, cs] = o_im
                    exit_wave[0, rows, cs] = w_re
                    exit_wave[1, rows, cs] = w_im
                    wave.append((w_re, w_im))
                waves.append(wave)
            for k in (0, 1):
                for part in (0, 1):
                    x0, x1 = waves[0][k][part], waves[1][k][part]
                    put(part * H + i, k * LANES, x0 + x1)
                    put(W + part * H + i, k * LANES, x0 - x1)
        left_dot(even, 0)
        left_dot(odd, 1)
        yield

        for branch in (0, 1):
            for i in range(0, H, step):
                for part in (0, 1):
                    rows = pl.ds(branch * W + part * H + i, step)
                    x0, x1 = wide[rows, 0:LANES], wide[rows, LANES:W]
                    put(branch * H + i, part * LANES, x0 + x1)
                    put(W + branch * H + i, part * LANES, x0 - x1)
        right_dot(even_t, 0)
        right_dot(odd_t, 1)
        yield

        for branch in (0, 1):
            for i in range(0, W, step):
                rows = pl.ds(branch * W + i, step)
                z_re, z_im = wide[rows, 0:LANES], wide[rows, LANES:W]
                power = z_re * z_re + z_im * z_im
                factor = amp[p, pl.ds(i, step), pl.ds(branch * LANES, LANES)] * lax.rsqrt(
                    jnp.maximum(power, FLOOR * FLOOR)
                )
                put(branch * W + i, 0, z_re * factor)
                put(branch * W + i, LANES, z_im * factor)
        right_dot(even, 0)
        right_dot(odd, 1)
        yield

        for branch in (0, 1):
            for i in range(0, H, step):
                rows_e = pl.ds(branch * H + i, step)
                rows_o = pl.ds(W + branch * H + i, step)
                for part in (0, 1):
                    cs = pl.ds(part * LANES, LANES)
                    x0, x1 = wide[rows_e, cs], wide[rows_o, cs]
                    put(branch * W + part * H + i, 0, x0 + x1)
                    put(branch * W + part * H + i, LANES, x0 - x1)
        left_dot(even_t, 0)
        left_dot(odd_t, 1)
        yield

        for i in range(0, H, step):
            for half in (0, 1):
                rows = pl.ds(half * H + i, step)
                turned = [[], []]
                for k in (0, 1):
                    cs = pl.ds(k * LANES, LANES)
                    back = []
                    for part in (0, 1):
                        x0 = wide[pl.ds(part * H + i, step), cs]
                        x1 = wide[pl.ds(W + part * H + i, step), cs]
                        back.append(x0 + x1 if half == 0 else x0 - x1)
                    d_re = live * (back[0] - exit_wave[0, rows, cs])
                    d_im = live * (back[1] - exit_wave[1, rows, cs])
                    o_re, o_im = window[0, rows, cs], window[1, rows, cs]
                    grads[0, rows, cs] += o_re * d_re + o_im * d_im
                    grads[1, rows, cs] += o_re * d_im - o_im * d_re
                    grads[2, rows, cs] += live * (o_re * o_re + o_im * o_im)
                    p_re, p_im = probe[0, rows, cs], probe[1, rows, cs]
                    turned[0].append(pltpu.roll(p_re * d_re + p_im * d_im, forth_turn, 1))
                    turned[1].append(pltpu.roll(p_re * d_im - p_im * d_re, forth_turn, 1))
                at = pl.ds(r + half * H + i, step)
                for part in (0, 1):
                    t0, t1 = turned[part]
                    total[part, ct, at, :] += jnp.where(lane >= s, t0, 0.0)
                    total[part, ct + 1, at, :] += jnp.where(lane >= s, t1, t0)
                    total[part, ct + 2, at, :] += jnp.where(lane < s, t1, 0.0)

    def pair(q, carry):
        for z in (0, 1):
            pltpu.make_async_copy(amp_in.at[2 * q + z], amp.at[2 * q + z], amp_sems.at[2 * q + z]).wait()

        @pl.when((alive[2 * q] != 0) | (alive[2 * q + 1] != 0))
        def _():
            runs = [slot(2 * q, 0), slot(2 * q + 1, 1)]
            for _ in range(5):
                for run in runs:
                    next(run, None)

        return carry

    lax.fori_loop(0, SLOTS // 2, pair, 0)
    depth = s_left.shape[1]
    mid = pl.ds(2 * H, W)
    outs = run_copies(
        [
            (total.at[:, :, pl.ds(H + TILE, H)], u_bottom),
            (total.at[:, :, pl.ds(0, H)], u_top),
            (total.at[:, pl.ds(EXT_TILES - depth, depth), mid], s_right),
            (total.at[:, pl.ds(0, depth), mid], s_left),
            (total.at[:, :, pl.ds(H, TILE)], u_mid),
        ],
        out_sems,
    )
    for h in (0, 1):
        for k in range(CHUNKS):
            rows = pl.ds(h * H + 4 * (k // 2), 4)
            cs = pl.ds((k % 2) * LANES, LANES)
            for plane in range(3):
                pack[h, k, pl.ds(4 * plane, 4), :] = grads[plane, rows, cs]
            pack[h, k, pl.ds(12, 4), :] = jnp.zeros((4, LANES), F32)
    outs += run_copies([(pack.at[half], keep), (pack.at[1 - half], give)], sems)
    for copy in outs:
        copy.wait()


ANY = pl.BlockSpec(memory_space=pl.ANY)
HBM = pl.BlockSpec(memory_space=pltpu.HBM)


def sweep(first, corners, alive, objects, probe, amp, tables):
    flops = SLOTS * 24 * 2 * W**3
    depth = 2 if first else 1
    strip = pltpu.HBM((2, depth, W, LANES), F32)
    margin = pltpu.HBM((2, EXT_TILES, H, LANES), F32)
    whole = pltpu.VMEM((2, EXT_TILES, EXT, LANES), F32)
    return pl.pallas_call(
        functools.partial(sweep_kernel, first),
        out_shape=(
            pltpu.HBM((2, EXT_TILES, TILE, LANES), F32),
            jax.ShapeDtypeStruct((2, W, W), F32),
            margin,
            margin,
            strip,
            strip,
            pltpu.HBM((CHUNKS, 16, LANES), F32),
            pltpu.HBM((CHUNKS, 16, LANES), F32),
        ),
        in_specs=[SMEM, SMEM] + [HBM] * len(objects) + [HBM] * (len(probe) + 2),
        out_specs=(HBM, VMEM) + (HBM,) * 6,
        scratch_shapes=[
            whole,
            whole,
            pltpu.VMEM((2, CHUNKS, 16, LANES), F32),
            pltpu.VMEM((SLOTS, W, W), F32),
            pltpu.VMEM((4, 2, W, W), BF16),
            pltpu.VMEM((2, 2, W, W), F32),
            pltpu.VMEM((2, 2, W, W), F32),
            pltpu.VMEM((3, W, W), F32),
            pltpu.VMEM((2, 2 * W, W), BF16),
            pltpu.VMEM((2, 2 * W, W), BF16),
            pltpu.VMEM((2, 2 * W, W), F32),
            pltpu.SemaphoreType.DMA((FIRST_COPIES if first else LATER_COPIES,)),
            pltpu.SemaphoreType.DMA((SLOTS,)),
            pltpu.SemaphoreType.DMA((3,)),
            pltpu.SemaphoreType.DMA((5,)),
            pltpu.VMEM((2, CHUNKS, 8, LANES), F32),
        ],
        compiler_params=pltpu.CompilerParams(vmem_limit_bytes=28 << 20),
        cost_estimate=pl.CostEstimate(flops=flops, bytes_accessed=16 << 20, transcendentals=SLOTS * W * W),
        name="sweep",
    )(corners, alive, *objects, *probe, in_hbm(amp), in_hbm(tables))


ROWS = ((0, H), (H, H + W), (H + W, TILE))


def object_tile(base, total, down, up, weight, mid, edge, put):
    for plane in (0, 1):
        parts = [
            total[plane, 0, 0:H, :] + down[plane, 0],
            total[plane, 0, H : H + W, :],
            total[plane, 0, H + W : TILE, :] + up[plane, 0],
        ]
        if mid is not None:
            parts = [parts[0] + edge[plane, 0, 0:H, :], parts[1] + mid[plane, 0], parts[2] + edge[plane, 0, H:W, :]]
        elif edge is not None:
            parts = [parts[n] + edge[plane, 0, a:b, :] for n, (a, b) in enumerate(ROWS)]
        for n, (a, b) in enumerate(ROWS):
            put(plane, n, base(plane, a, b) + parts[n] * weight[0, a:b, :])


def rows_kernel(tiles, lefts, rights, totals, weights, s_left, s_right, folds, outs):
    k = pl.program_id(0)

    def run(bases, strip):
        for n in (0, 1):
            for plane in (0, 1):
                part = totals[n][plane, 0]
                if folds:
                    part = part + folds[n][plane, 0]
                if strip is not None:
                    part = part + strip[plane, 0, n * H : (n + 1) * H, :]
                outs[n][plane, 0] = bases[n][plane] + part * weights[n][0]

    last = EXT_TILES - 1
    pl.when(k == 0)(lambda: run(lefts, s_left))
    pl.when(k == 1)(lambda: run(tiles, s_left))
    pl.when((k > 1) & (k < last - 1))(lambda: run(tiles, None))
    pl.when(k == last - 1)(lambda: run(tiles, s_right))
    pl.when(k == last)(lambda: run(rights, s_right))


def edge_rows_kernel(t0, t1, l0, l1, r0, r1, u0, u1, w0, w1, s_left, s_right, down, up, o0, o1):
    rows_kernel((t0, t1), (l0, l1), (r0, r1), (u0, u1), (w0, w1), s_left, s_right, (down, up), (o0, o1))


def mid_rows_kernel(t0, t1, l0, l1, r0, r1, u0, u1, w0, w1, s_left, s_right, o0, o1):
    rows_kernel((t0, t1), (l0, l1), (r0, r1), (u0, u1), (w0, w1), s_left, s_right, (), (o0, o1))


def last_kernel(half, mine, other, m0, m1, m2, m3, total, down, up, e_left, e_right, weight, out, probe, halves):
    k = pl.program_id(0)

    @pl.when(k == 0)
    def _():
        halves[half[0]] = mine[...]
        halves[1 - half[0]] = other[...]
        unpack_probe((halves.at[0], halves.at[1]), probe)

    def put(plane, n, value):
        a, b = ROWS[n]
        out[plane, a:b, :] = value

    def base(plane, a, b):
        return jnp.concatenate([m[plane, 0] for m in (m0, m1, m2, m3)[a // H : b // H]], axis=0)

    def run(edge):
        object_tile(base, total, down, up, weight, None, edge, put)

    last = TILE // LANES - 1
    pl.when(k == 0)(lambda: run(e_left))
    pl.when((k > 0) & (k < last))(lambda: run(None))
    pl.when(k == last)(lambda: run(e_right))


def object_step(kernel, grid, in_specs, out_specs, out_shape, name, scratch, *args):
    return pl.pallas_call(
        kernel,
        grid=(grid,),
        out_shape=out_shape,
        in_specs=in_specs,
        out_specs=out_specs,
        scratch_shapes=scratch,
        compiler_params=pltpu.CompilerParams(vmem_limit_bytes=16 << 20),
        cost_estimate=pl.CostEstimate(flops=2 << 20, bytes_accessed=8 << 20, transcendentals=0),
        name=name,
    )(*args)


def tile_spec(rows, index, row=0):
    return pl.BlockSpec((2, 1, rows, LANES), lambda k: (0, index(k), row, 0))


def rows_step(kernel, blocks, specimen, left, right, total, weight, strips, folds, name):
    tiles = TILE // LANES
    specs = [pl.BlockSpec((2, H, LANES), lambda k, n=n: (0, n, jnp.clip(k - 1, 0, tiles - 1))) for n in blocks]
    specs += [pl.BlockSpec((2, H, LANES), lambda k, n=n: (0, n, 0)) for n in blocks] * 2
    specs += [tile_spec(H, lambda k: k, n) for n in blocks]
    specs += [pl.BlockSpec((1, H, LANES), lambda k, n=n: (k, n, 0)) for n in blocks]
    specs += [tile_spec(W, lambda k: jnp.minimum(k, 1)), tile_spec(W, lambda k: jnp.maximum(k - EXT_TILES + 2, 0))]
    specs += [tile_spec(H, lambda k: k) for _ in folds]
    specimen, total, weight = in_hbm(specimen), in_hbm(total), in_hbm(weight)
    return object_step(
        kernel,
        EXT_TILES,
        specs,
        (tile_spec(H, lambda k: k),) * 2,
        (pltpu.HBM((2, EXT_TILES, H, LANES), F32),) * 2,
        name,
        [],
        *[x for x in (specimen, left, right, total, weight) for _ in blocks],
        *strips,
        *folds,
    )


def last_step(half, chunks, rows, terms, weight):
    tiles = TILE // LANES
    total, *folds, e_left, e_right = terms
    whole = pl.BlockSpec((CHUNKS, 8, LANES), lambda k: (0, 0, 0))
    specs = [SMEM, whole, whole] + [tile_spec(H, lambda k: k + 1)] * 4 + [tile_spec(TILE, lambda k: k + 1)]
    specs += [tile_spec(H, lambda k: k + 1)] * 2 + [tile_spec(TILE, lambda k: 0)] * 2
    specs += [pl.BlockSpec((1, TILE, LANES), lambda k: (k + 1, 0, 0))]
    return object_step(
        last_kernel,
        tiles,
        specs,
        (pl.BlockSpec((2, TILE, LANES), lambda k: (0, 0, k)), pl.BlockSpec((2, W, W), lambda k: (0, 0, 0))),
        (jax.ShapeDtypeStruct((2, TILE, TILE), F32), jax.ShapeDtypeStruct((2, W, W), F32)),
        "last",
        [pltpu.VMEM((2, CHUNKS, 8, LANES), F32)],
        half,
        *chunks,
        *[in_hbm(x) for x in rows],
        in_hbm(total),
        *folds,
        e_left,
        e_right,
        in_hbm(weight),
    )


PAD_ROWS = TILE + 2 * W
PAD_TILES = (EXT + 2 * W) // LANES


def light_kernel(spots, probe, weight, density, field):
    density[...] = probe[0] * probe[0] + probe[1] * probe[1]
    field[...] = jnp.zeros_like(field)
    step = 16
    lane = lax.broadcasted_iota(jnp.int32, (step, LANES), 1)

    def spot(q, carry):
        r, c, on = spots[3 * q], spots[3 * q + 1], spots[3 * q + 2]

        @pl.when((on != 0) & (r > 0) & (r < W + TILE) & (c > 0) & (c < W + EXT))
        def _():
            ct = jnp.minimum(c // LANES, PAD_TILES - 3)
            s = c - ct * LANES
            turn = lax.rem(s, LANES)
            for i in range(0, W, step):
                at = pl.ds(r + i, step)
                t0 = pltpu.roll(density[pl.ds(i, step), 0:LANES], turn, 1)
                t1 = pltpu.roll(density[pl.ds(i, step), LANES:W], turn, 1)
                field[ct, at, :] += jnp.where(lane >= s, t0, 0.0)
                field[ct + 1, at, :] += jnp.where(lane >= s, t1, t0)
                field[ct + 2, at, :] += jnp.where(lane < s, t1, 0.0)

        return carry

    lax.fori_loop(0, spots.shape[0] // 3, spot, 0)
    for k in range(EXT_TILES):
        weight[k] = 1.0 / (field[W // LANES + k, W : W + TILE, :] + SPECIMEN_REG)


def light(spots, probe):
    return pl.pallas_call(
        light_kernel,
        out_shape=pltpu.HBM((EXT_TILES, TILE, LANES), F32),
        in_specs=[SMEM, VMEM],
        out_specs=VMEM,
        scratch_shapes=[pltpu.VMEM((W, W), F32), pltpu.VMEM((PAD_TILES, PAD_ROWS, LANES), F32)],
        compiler_params=pltpu.CompilerParams(vmem_limit_bytes=12 << 20),
        cost_estimate=pl.CostEstimate(flops=20 << 20, bytes_accessed=20 << 20, transcendentals=0),
        name="light",
    )(spots, probe)


def shift(value, axis, by):
    length = lax.axis_size(axis)
    pairs = [(i, i + by) for i in range(length) if 0 <= i + by < length]
    return lax.ppermute(value, axis, pairs)


def sibling(value):
    return lax.ppermute(value, "ty", [(i, i ^ 1) for i in range(lax.axis_size("ty"))])


def in_hbm(value):
    return pltpu.with_memory_space_constraint(value, pltpu.HBM)


def exchange(value):
    rows, columns = lax.axis_size("ty"), lax.axis_size("tx")
    groups = [[i * columns + j for i in range(parity, rows, 2) for j in range(columns)] for parity in (0, 1)]
    return lax.all_to_all(value, BOTH, 0, 0, tiled=True, axis_index_groups=groups)


def probe_step(mine, probe):
    ty, tx = lax.axis_index("ty"), lax.axis_index("tx")
    half, chunk = ty % 2, (ty // 2) * lax.axis_size("tx") + tx
    mine = mine.reshape(CHUNKS, 16, LANES).sum(axis=0)
    start = (0, half * H + 4 * (chunk // 2), LANES * (chunk % 2))
    own = lax.dynamic_slice(probe, start, (2, 4, LANES)).reshape(8, LANES)
    denominator = mine[8:12] + PROBE_REG
    new = own + mine[0:8] / jnp.concatenate([denominator, denominator])
    return jnp.broadcast_to(new, (CHUNKS, 8, LANES)).reshape(CHUNKS * 8, LANES)


def edges(total, down, up, depth, split):
    def strip(lo, hi):
        parts = [total[:, lo:hi, :H] + down[:, lo:hi], total[:, lo:hi, H + W :] + up[:, lo:hi]]
        if not split:
            parts.insert(1, total[:, lo:hi, H : H + W])
        return jnp.concatenate(parts, axis=2)

    return strip(0, depth), strip(EXT_TILES - depth, EXT_TILES)


def finish(swept, probe, weight):
    total, _, u_top, u_bottom, s_left, s_right, keep, give = swept
    depth = s_left.shape[1]
    split = depth > 1
    sums = (keep + sibling(give)).reshape(CHUNKS * 16, LANES)
    down = shift(u_bottom, "ty", 1)
    up = shift(u_top, "ty", -1)
    m_left = shift(s_right, "tx", 1) if split else None
    m_right = shift(s_left, "tx", -1) if split else None
    mine = exchange(sums)
    down, up, m_left, m_right, mine, weight = lax.optimization_barrier((down, up, m_left, m_right, mine, weight))
    low, high = edges(total, down, up, depth, split)
    e_left = shift(high, "tx", 1)
    e_right = shift(low, "tx", -1)
    chunks = exchange(probe_step(mine, probe))
    e_left, e_right, chunks = lax.optimization_barrier((e_left, e_right, chunks))
    chunks = chunks.reshape(CHUNKS, 8, LANES)
    strips = (m_left, m_right, e_left, e_right) if split else (e_left, e_right)
    return (chunks, sibling(chunks)), (total, down, up) + strips, weight


def body(specimen, probe_field, intensity, positions, occupied_slots):
    ty, tx = lax.axis_index("ty"), lax.axis_index("tx")
    row_start = ty * TILE - H
    column_start = tx * TILE - H
    corners = positions - jnp.stack([row_start, column_start])[None, :]
    tables = jnp.asarray(dft_tables())
    half = (ty % 2).reshape(1)
    alive = jnp.concatenate([occupied_slots, half])

    slots = jnp.concatenate([positions, occupied_slots[:, None]], axis=1).astype(F32)
    tag = jnp.pad(slots, ((0, 0), (0, LANES - 3)))
    both = jnp.broadcast_to(tag, (2, SLOTS, LANES))
    left = shift(jnp.concatenate([specimen[:, :, TILE - H :], both], axis=1), "tx", 1)
    right = shift(jnp.concatenate([specimen[:, :, :H], both], axis=1), "tx", -1)
    top = shift(specimen[:, TILE - H :, :], "ty", 1)
    bottom = shift(specimen[:, :H, :], "ty", -1)
    amp = prepare(intensity)
    left, right, top, bottom, amp = lax.optimization_barrier((left, right, top, bottom, amp))
    sides = jnp.stack([left, right], axis=1)
    tags = jnp.stack([sides[0, :, TILE:, :], both])
    corner_top = shift(jnp.concatenate([sides[:, :, TILE - H : TILE, :], tags], axis=2), "ty", 1)
    corner_bottom = shift(jnp.concatenate([sides[:, :, :H, :], tags], axis=2), "ty", -1)

    objects = (in_hbm(specimen), left, right, top, bottom, corner_top, corner_bottom)
    swept = sweep(True, corners, alive, objects, (probe_field,), amp, tables)

    lines = [x[:, :, -SLOTS:, :3].reshape(4, SLOTS, 3)[:3] for x in (corner_top, tags, corner_bottom)]
    around = jnp.concatenate(lines).reshape(9 * SLOTS, 3).astype(jnp.int32)
    spots = (around - jnp.stack([ty * TILE - W, column_start - W, 0])[None, :]).reshape(-1)
    weight = light(spots, probe_field)

    chunks, terms, weight = finish(swept, probe_field, weight)
    total, down, up, m_left, m_right, e_left, e_right = terms
    first_rows, last_rows = rows_step(
        edge_rows_kernel, (0, 3), specimen, left, right, total, weight, (e_left, e_right), (down, up), "edge_rows"
    )
    top = shift(last_rows, "ty", 1)
    bottom = shift(first_rows, "ty", -1)
    mid_rows = rows_step(
        mid_rows_kernel, (1, 2), specimen, left, right, total, weight, (m_left, m_right), (), "mid_rows"
    )
    rows = (first_rows, *mid_rows, last_rows)

    swept = sweep(False, corners, alive, tuple(in_hbm(x) for x in rows) + (top, bottom), chunks, amp, tables)
    probe_field = swept[1]
    weight = light(spots, probe_field)
    chunks, terms, weight = finish(swept, probe_field, weight)
    return last_step(half, chunks, rows, terms, weight)


def solution(mesh):
    return jax.shard_map(
        body,
        mesh=mesh,
        in_specs=(
            P(None, "ty", "tx"),
            P(),
            P(BOTH, None, None),
            P(BOTH, None),
            P(BOTH),
        ),
        out_specs=(P(None, "ty", "tx"), P()),
        check_vma=False,
    )
```

```python
import functools
import math

import jax
import jax.numpy as jnp
import numpy as np
from jax import lax
from jax.experimental import pallas as pl
from jax.experimental.pallas import tpu as pltpu
from jax.sharding import PartitionSpec as P

FLOOR = 0.2
SPECIMEN_REG = 0.5
PROBE_REG = 1.0

W = 256
H = W // 2
TILE = 512
EXT = TILE + 2 * H
SLOTS = 8
LANES = 128
EXT_TILES = EXT // LANES
CHUNKS = 64
BOTH = ("ty", "tx")
F32 = jnp.float32
BF16 = jnp.bfloat16
VMEM = pl.BlockSpec(memory_space=pltpu.VMEM)
SMEM = pl.BlockSpec(memory_space=pltpu.SMEM)


def dft_tables():
    j = np.arange(H)[:, None]
    m = np.arange(H)[None, :]
    parts = []
    for odd in (0, 1):
        phase = -2.0 * np.pi * ((m * (2 * j + odd)) % W) / W
        re, im = np.cos(phase) / math.sqrt(W), np.sin(phase) / math.sqrt(W)
        full = np.block([[re, -im], [im, re]])
        for mat in (full, full.T):
            hi = mat.astype(jnp.bfloat16)
            lo = (mat - hi.astype(np.float64)).astype(jnp.bfloat16)
            parts.append(np.stack([hi, lo]))
    return np.stack(parts)


def column_order():
    pick = np.zeros((W, W), np.float32)
    for k in range(H):
        pick[2 * k, k] = 1.0
        pick[2 * k + 1, H + k] = 1.0
    return pick.astype(jnp.bfloat16)


def split2(x):
    hi = x.astype(BF16)
    return hi, (x - hi.astype(F32)).astype(BF16)


def dot(a, b):
    return jnp.dot(a, b, preferred_element_type=F32)


def split3(x):
    hi = x.astype(BF16)
    return (hi,) + split2(x - hi.astype(F32))


def prep_kernel(intensity, pick, pick_t, amp):
    def slot(p, carry):
        hi, mid, lo = split3(jnp.sqrt(intensity[p]))
        x = dot(lo, pick[...]) + dot(mid, pick[...]) + dot(hi, pick[...])
        hi, mid, lo = split3(x)
        amp[p] = dot(pick_t[...], lo) + dot(pick_t[...], mid) + dot(pick_t[...], hi)
        return carry

    lax.fori_loop(0, SLOTS, slot, 0)


def prepare(intensity):
    pick = column_order()
    return pl.pallas_call(
        prep_kernel,
        out_shape=pltpu.HBM((SLOTS, W, W), F32),
        in_specs=[VMEM, VMEM, VMEM],
        out_specs=VMEM,
        cost_estimate=pl.CostEstimate(flops=4 * 3 * SLOTS * W**3, bytes_accessed=16 * SLOTS * W * W, transcendentals=SLOTS * W * W),
        name="amplitudes",
    )(intensity, jnp.asarray(pick), jnp.asarray(pick.T))


def run_copies(pairs, sems):
    copies = [pltpu.make_async_copy(src, dst, sems.at[n]) for n, (src, dst) in enumerate(pairs)]
    for copy in copies:
        copy.start()
    return copies


def first_loads(refs, ext):
    tile, left, right, top, bottom, corner_top, corner_bottom = refs
    inner, upper, lower = pl.ds(H, TILE), pl.ds(0, H), pl.ds(H + TILE, H)
    last = EXT_TILES - 1
    pairs = [
        (left.at[:, pl.ds(0, TILE)], ext.at[:, 0, inner]),
        (right.at[:, pl.ds(0, TILE)], ext.at[:, last, inner]),
        (corner_top.at[0, :, pl.ds(0, H)], ext.at[:, 0, upper]),
        (corner_top.at[1, :, pl.ds(0, H)], ext.at[:, last, upper]),
        (corner_bottom.at[0, :, pl.ds(0, H)], ext.at[:, 0, lower]),
        (corner_bottom.at[1, :, pl.ds(0, H)], ext.at[:, last, lower]),
    ]
    for k in range(TILE // LANES):
        cs = pl.ds(k * LANES, LANES)
        pairs.append((tile.at[:, :, cs], ext.at[:, 1 + k, inner]))
        pairs.append((top.at[:, :, cs], ext.at[:, 1 + k, upper]))
        pairs.append((bottom.at[:, :, cs], ext.at[:, 1 + k, lower]))
    return pairs


def later_loads(refs, ext):
    *rows, top, bottom = refs
    return [(x, ext.at[:, :, pl.ds(H * (n + 1), H)]) for n, x in enumerate(rows)] + [
        (top, ext.at[:, :, pl.ds(0, H)]),
        (bottom, ext.at[:, :, pl.ds(H + TILE, H)]),
    ]


FIRST_COPIES = 18
LATER_COPIES = 6


def unpack_probe(halves, probe):
    for h, chunks in enumerate(halves):
        for k in range(CHUNKS):
            rows = pl.ds(h * H + 4 * (k // 2), 4)
            cs = pl.ds((k % 2) * LANES, LANES)
            probe[0, rows, cs] = chunks[k, 0:4, :]
            probe[1, rows, cs] = chunks[k, 4:8, :]


def sweep_kernel(first, corners, alive, *refs):
    n, m = (7, 1) if first else (6, 2)
    objects, probe_in, (amp_in, tables_in) = refs[:n], refs[n : n + m], refs[n + m : n + m + 2]
    rest = refs[n + m + 2 :]
    half = alive[SLOTS]
    u_mid, probe, u_top, u_bottom, s_left, s_right, keep, give = rest[:8]
    total, ext, pack, amp, tables, windows, exit_waves, grads, his, los, wides, ext_sems, amp_sems, sems, out_sems, halves = rest[8:]
    loads = first_loads if first else later_loads
    copies = run_copies(loads(objects, ext), ext_sems)
    more = [(tables_in, tables)]
    if first:
        more.append((probe_in[0], probe))
    else:
        more += [(probe_in[0], halves.at[half]), (probe_in[1], halves.at[1 - half])]
    copies += run_copies(more, sems)
    run_copies([(amp_in.at[p], amp.at[p]) for p in range(SLOTS)], amp_sems)
    total[...] = jnp.zeros_like(total)
    grads[...] = jnp.zeros_like(grads)
    even, even_t, odd, odd_t = 0, 1, 2, 3
    step = 16
    lane = lax.broadcasted_iota(jnp.int32, (step, LANES), 1)
    for copy in copies:
        copy.wait()
    if not first:
        unpack_probe((halves.at[0], halves.at[1]), probe)

    def slot(p, z):
        window, exit_wave = windows.at[z], exit_waves.at[z]
        a_hi, a_lo, wide = his.at[z], los.at[z], wides.at[z]

        def left_dot(t, branch):
            rows = pl.ds(branch * W, W)
            hi, lo = a_hi[rows, :], a_lo[rows, :]
            wide[rows, :] = dot(tables[t, 0], hi) + dot(tables[t, 1], hi) + dot(tables[t, 0], lo)

        def right_dot(t, branch):
            rows = pl.ds(branch * W, W)
            hi, lo = a_hi[rows, :], a_lo[rows, :]
            wide[rows, :] = dot(hi, tables[t, 0]) + dot(hi, tables[t, 1]) + dot(lo, tables[t, 0])

        def put(row, col, value):
            hi, lo = split2(value)
            a_hi[pl.ds(row, step), pl.ds(col, LANES)] = hi
            a_lo[pl.ds(row, step), pl.ds(col, LANES)] = lo

        live = alive[p].astype(F32)
        r = corners[p, 0]
        c = corners[p, 1]
        ct = jnp.minimum(c // LANES, EXT_TILES - 3)
        s = c - ct * LANES
        back_turn = lax.rem(LANES - s, LANES)
        forth_turn = lax.rem(s, LANES)

        for i in range(0, H, step):
            waves = []
            for half in (0, 1):
                parts = []
                for plane in (0, 1):
                    turned = [
                        pltpu.roll(ext[plane, ct + k, pl.ds(r + half * H + i, step), :], back_turn, 1)
                        for k in range(3)
                    ]
                    cols = [jnp.where(lane < LANES - s, turned[k], turned[k + 1]) for k in (0, 1)]
                    parts.append(cols)
                rows = pl.ds(half * H + i, step)
                wave = []
                for k in (0, 1):
                    cs = pl.ds(k * LANES, LANES)
                    o_re, o_im = parts[0][k], parts[1][k]
                    p_re, p_im = probe[0, rows, cs], probe[1, rows, cs]
                    w_re = p_re * o_re - p_im * o_im
                    w_im = p_re * o_im + p_im * o_re
                    window[0, rows, cs] = o_re
                    window[1, rows, cs] = o_im
                    exit_wave[0, rows, cs] = w_re
                    exit_wave[1, rows, cs] = w_im
                    wave.append((w_re, w_im))
                waves.append(wave)
            for k in (0, 1):
                for part in (0, 1):
                    x0, x1 = waves[0][k][part], waves[1][k][part]
                    put(part * H + i, k * LANES, x0 + x1)
                    put(W + part * H + i, k * LANES, x0 - x1)
        left_dot(even, 0)
        left_dot(odd, 1)
        yield

        for branch in (0, 1):
            for i in range(0, H, step):
                for part in (0, 1):
                    rows = pl.ds(branch * W + part * H + i, step)
                    x0, x1 = wide[rows, 0:LANES], wide[rows, LANES:W]
                    put(branch * H + i, part * LANES, x0 + x1)
                    put(W + branch * H + i, part * LANES, x0 - x1)
        right_dot(even_t, 0)
        right_dot(odd_t, 1)
        yield

        for branch in (0, 1):
            for i in range(0, W, step):
                rows = pl.ds(branch * W + i, step)
                z_re, z_im = wide[rows, 0:LANES], wide[rows, LANES:W]
                power = z_re * z_re + z_im * z_im
                factor = amp[p, pl.ds(i, step), pl.ds(branch * LANES, LANES)] * lax.rsqrt(
                    jnp.maximum(power, FLOOR * FLOOR)
                )
                put(branch * W + i, 0, z_re * factor)
                put(branch * W + i, LANES, z_im * factor)
        right_dot(even, 0)
        right_dot(odd, 1)
        yield

        for branch in (0, 1):
            for i in range(0, H, step):
                rows_e = pl.ds(branch * H + i, step)
                rows_o = pl.ds(W + branch * H + i, step)
                for part in (0, 1):
                    cs = pl.ds(part * LANES, LANES)
                    x0, x1 = wide[rows_e, cs], wide[rows_o, cs]
                    put(branch * W + part * H + i, 0, x0 + x1)
                    put(branch * W + part * H + i, LANES, x0 - x1)
        left_dot(even_t, 0)
        left_dot(odd_t, 1)
        yield

        for i in range(0, H, step):
            for half in (0, 1):
                rows = pl.ds(half * H + i, step)
                turned = [[], []]
                for k in (0, 1):
                    cs = pl.ds(k * LANES, LANES)
                    back = []
                    for part in (0, 1):
                        x0 = wide[pl.ds(part * H + i, step), cs]
                        x1 = wide[pl.ds(W + part * H + i, step), cs]
                        back.append(x0 + x1 if half == 0 else x0 - x1)
                    d_re = live * (back[0] - exit_wave[0, rows, cs])
                    d_im = live * (back[1] - exit_wave[1, rows, cs])
                    o_re, o_im = window[0, rows, cs], window[1, rows, cs]
                    grads[0, rows, cs] += o_re * d_re + o_im * d_im
                    grads[1, rows, cs] += o_re * d_im - o_im * d_re
                    grads[2, rows, cs] += live * (o_re * o_re + o_im * o_im)
                    p_re, p_im = probe[0, rows, cs], probe[1, rows, cs]
                    turned[0].append(pltpu.roll(p_re * d_re + p_im * d_im, forth_turn, 1))
                    turned[1].append(pltpu.roll(p_re * d_im - p_im * d_re, forth_turn, 1))
                at = pl.ds(r + half * H + i, step)
                for part in (0, 1):
                    t0, t1 = turned[part]
                    total[part, ct, at, :] += jnp.where(lane >= s, t0, 0.0)
                    total[part, ct + 1, at, :] += jnp.where(lane >= s, t1, t0)
                    total[part, ct + 2, at, :] += jnp.where(lane < s, t1, 0.0)

    def pair(q, carry):
        for z in (0, 1):
            pltpu.make_async_copy(amp_in.at[2 * q + z], amp.at[2 * q + z], amp_sems.at[2 * q + z]).wait()

        @pl.when((alive[2 * q] != 0) | (alive[2 * q + 1] != 0))
        def _():
            runs = [slot(2 * q, 0), slot(2 * q + 1, 1)]
            for _ in range(5):
                for run in runs:
                    next(run, None)

        return carry

    lax.fori_loop(0, SLOTS // 2, pair, 0)
    depth = s_left.shape[1]
    mid = pl.ds(2 * H, W)
    outs = run_copies(
        [
            (total.at[:, :, pl.ds(H + TILE, H)], u_bottom),
            (total.at[:, :, pl.ds(0, H)], u_top),
            (total.at[:, pl.ds(EXT_TILES - depth, depth), mid], s_right),
            (total.at[:, pl.ds(0, depth), mid], s_left),
            (total.at[:, :, pl.ds(H, TILE)], u_mid),
        ],
        out_sems,
    )
    for h in (0, 1):
        for k in range(CHUNKS):
            rows = pl.ds(h * H + 4 * (k // 2), 4)
            cs = pl.ds((k % 2) * LANES, LANES)
            for plane in range(3):
                pack[h, k, pl.ds(4 * plane, 4), :] = grads[plane, rows, cs]
            pack[h, k, pl.ds(12, 4), :] = jnp.zeros((4, LANES), F32)
    outs += run_copies([(pack.at[half], keep), (pack.at[1 - half], give)], sems)
    for copy in outs:
        copy.wait()


ANY = pl.BlockSpec(memory_space=pl.ANY)
HBM = pl.BlockSpec(memory_space=pltpu.HBM)


def sweep(first, corners, alive, objects, probe, amp, tables):
    flops = SLOTS * 24 * 2 * W**3
    depth = 2 if first else 1
    strip = pltpu.HBM((2, depth, W, LANES), F32)
    margin = pltpu.HBM((2, EXT_TILES, H, LANES), F32)
    whole = pltpu.VMEM((2, EXT_TILES, EXT, LANES), F32)
    return pl.pallas_call(
        functools.partial(sweep_kernel, first),
        out_shape=(
            pltpu.HBM((2, EXT_TILES, TILE, LANES), F32),
            jax.ShapeDtypeStruct((2, W, W), F32),
            margin,
            margin,
            strip,
            strip,
            pltpu.HBM((CHUNKS, 16, LANES), F32),
            pltpu.HBM((CHUNKS, 16, LANES), F32),
        ),
        in_specs=[SMEM, SMEM] + [HBM] * len(objects) + [HBM] * (len(probe) + 2),
        out_specs=(HBM, VMEM) + (HBM,) * 6,
        scratch_shapes=[
            whole,
            whole,
            pltpu.VMEM((2, CHUNKS, 16, LANES), F32),
            pltpu.VMEM((SLOTS, W, W), F32),
            pltpu.VMEM((4, 2, W, W), BF16),
            pltpu.VMEM((2, 2, W, W), F32),
            pltpu.VMEM((2, 2, W, W), F32),
            pltpu.VMEM((3, W, W), F32),
            pltpu.VMEM((2, 2 * W, W), BF16),
            pltpu.VMEM((2, 2 * W, W), BF16),
            pltpu.VMEM((2, 2 * W, W), F32),
            pltpu.SemaphoreType.DMA((FIRST_COPIES if first else LATER_COPIES,)),
            pltpu.SemaphoreType.DMA((SLOTS,)),
            pltpu.SemaphoreType.DMA((3,)),
            pltpu.SemaphoreType.DMA((5,)),
            pltpu.VMEM((2, CHUNKS, 8, LANES), F32),
        ],
        compiler_params=pltpu.CompilerParams(vmem_limit_bytes=28 << 20),
        cost_estimate=pl.CostEstimate(flops=flops, bytes_accessed=16 << 20, transcendentals=SLOTS * W * W),
        name="sweep",
    )(corners, alive, *objects, *probe, in_hbm(amp), in_hbm(tables))


ROWS = ((0, H), (H, H + W), (H + W, TILE))


def object_tile(base, total, down, up, weight, mid, edge, put):
    for plane in (0, 1):
        parts = [
            total[plane, 0, 0:H, :] + down[plane, 0],
            total[plane, 0, H : H + W, :],
            total[plane, 0, H + W : TILE, :] + up[plane, 0],
        ]
        if mid is not None:
            parts = [parts[0] + edge[plane, 0, 0:H, :], parts[1] + mid[plane, 0], parts[2] + edge[plane, 0, H:W, :]]
        elif edge is not None:
            parts = [parts[n] + edge[plane, 0, a:b, :] for n, (a, b) in enumerate(ROWS)]
        for n, (a, b) in enumerate(ROWS):
            put(plane, n, base(plane, a, b) + parts[n] * weight[0, a:b, :])


def rows_kernel(tiles, lefts, rights, totals, weights, s_left, s_right, folds, outs):
    k = pl.program_id(0)

    def run(bases, strip):
        for n in (0, 1):
            for plane in (0, 1):
                part = totals[n][plane, 0]
                if folds:
                    part = part + folds[n][plane, 0]
                if strip is not None:
                    part = part + strip[plane, 0, n * H : (n + 1) * H, :]
                outs[n][plane, 0] = bases[n][plane] + part * weights[n][0]

    last = EXT_TILES - 1
    pl.when(k == 0)(lambda: run(lefts, s_left))
    pl.when(k == 1)(lambda: run(tiles, s_left))
    pl.when((k > 1) & (k < last - 1))(lambda: run(tiles, None))
    pl.when(k == last - 1)(lambda: run(tiles, s_right))
    pl.when(k == last)(lambda: run(rights, s_right))


def edge_rows_kernel(t0, t1, l0, l1, r0, r1, u0, u1, w0, w1, s_left, s_right, down, up, o0, o1):
    rows_kernel((t0, t1), (l0, l1), (r0, r1), (u0, u1), (w0, w1), s_left, s_right, (down, up), (o0, o1))


def mid_rows_kernel(t0, t1, l0, l1, r0, r1, u0, u1, w0, w1, s_left, s_right, o0, o1):
    rows_kernel((t0, t1), (l0, l1), (r0, r1), (u0, u1), (w0, w1), s_left, s_right, (), (o0, o1))


def last_kernel(half, mine, other, m0, m1, m2, m3, total, down, up, e_left, e_right, weight, out, probe, halves):
    k = pl.program_id(0)

    @pl.when(k == 0)
    def _():
        halves[half[0]] = mine[...]
        halves[1 - half[0]] = other[...]
        unpack_probe((halves.at[0], halves.at[1]), probe)

    def put(plane, n, value):
        a, b = ROWS[n]
        out[plane, a:b, :] = value

    def base(plane, a, b):
        return jnp.concatenate([m[plane, 0] for m in (m0, m1, m2, m3)[a // H : b // H]], axis=0)

    def run(edge):
        object_tile(base, total, down, up, weight, None, edge, put)

    last = TILE // LANES - 1
    pl.when(k == 0)(lambda: run(e_left))
    pl.when((k > 0) & (k < last))(lambda: run(None))
    pl.when(k == last)(lambda: run(e_right))


def object_step(kernel, grid, in_specs, out_specs, out_shape, name, scratch, *args):
    return pl.pallas_call(
        kernel,
        grid=(grid,),
        out_shape=out_shape,
        in_specs=in_specs,
        out_specs=out_specs,
        scratch_shapes=scratch,
        compiler_params=pltpu.CompilerParams(vmem_limit_bytes=16 << 20),
        cost_estimate=pl.CostEstimate(flops=2 << 20, bytes_accessed=8 << 20, transcendentals=0),
        name=name,
    )(*args)


def tile_spec(rows, index, row=0):
    return pl.BlockSpec((2, 1, rows, LANES), lambda k: (0, index(k), row, 0))


def rows_step(kernel, blocks, specimen, left, right, total, weight, strips, folds, name):
    tiles = TILE // LANES
    specs = [pl.BlockSpec((2, H, LANES), lambda k, n=n: (0, n, jnp.clip(k - 1, 0, tiles - 1))) for n in blocks]
    specs += [pl.BlockSpec((2, H, LANES), lambda k, n=n: (0, n, 0)) for n in blocks] * 2
    specs += [tile_spec(H, lambda k: k, n) for n in blocks]
    specs += [pl.BlockSpec((1, H, LANES), lambda k, n=n: (k, n, 0)) for n in blocks]
    specs += [tile_spec(W, lambda k: jnp.minimum(k, 1)), tile_spec(W, lambda k: jnp.maximum(k - EXT_TILES + 2, 0))]
    specs += [tile_spec(H, lambda k: k) for _ in folds]
    specimen, total, weight = in_hbm(specimen), in_hbm(total), in_hbm(weight)
    return object_step(
        kernel,
        EXT_TILES,
        specs,
        (tile_spec(H, lambda k: k),) * 2,
        (pltpu.HBM((2, EXT_TILES, H, LANES), F32),) * 2,
        name,
        [],
        *[x for x in (specimen, left, right, total, weight) for _ in blocks],
        *strips,
        *folds,
    )


def last_step(half, chunks, rows, terms, weight):
    tiles = TILE // LANES
    total, *folds, e_left, e_right = terms
    whole = pl.BlockSpec((CHUNKS, 8, LANES), lambda k: (0, 0, 0))
    specs = [SMEM, whole, whole] + [tile_spec(H, lambda k: k + 1)] * 4 + [tile_spec(TILE, lambda k: k + 1)]
    specs += [tile_spec(H, lambda k: k + 1)] * 2 + [tile_spec(TILE, lambda k: 0)] * 2
    specs += [pl.BlockSpec((1, TILE, LANES), lambda k: (k + 1, 0, 0))]
    return object_step(
        last_kernel,
        tiles,
        specs,
        (pl.BlockSpec((2, TILE, LANES), lambda k: (0, 0, k)), pl.BlockSpec((2, W, W), lambda k: (0, 0, 0))),
        (jax.ShapeDtypeStruct((2, TILE, TILE), F32), jax.ShapeDtypeStruct((2, W, W), F32)),
        "last",
        [pltpu.VMEM((2, CHUNKS, 8, LANES), F32)],
        half,
        *chunks,
        *[in_hbm(x) for x in rows],
        in_hbm(total),
        *folds,
        e_left,
        e_right,
        in_hbm(weight),
    )


PAD_ROWS = TILE + 2 * W
PAD_TILES = (EXT + 2 * W) // LANES


def light_kernel(spots, probe, weight, density, field):
    density[...] = probe[0] * probe[0] + probe[1] * probe[1]
    field[...] = jnp.zeros_like(field)
    step = 16
    lane = lax.broadcasted_iota(jnp.int32, (step, LANES), 1)

    def spot(q, carry):
        r, c, on = spots[3 * q], spots[3 * q + 1], spots[3 * q + 2]

        @pl.when((on != 0) & (r > 0) & (r < W + TILE) & (c > 0) & (c < W + EXT))
        def _():
            ct = jnp.minimum(c // LANES, PAD_TILES - 3)
            s = c - ct * LANES
            turn = lax.rem(s, LANES)
            for i in range(0, W, step):
                at = pl.ds(r + i, step)
                t0 = pltpu.roll(density[pl.ds(i, step), 0:LANES], turn, 1)
                t1 = pltpu.roll(density[pl.ds(i, step), LANES:W], turn, 1)
                field[ct, at, :] += jnp.where(lane >= s, t0, 0.0)
                field[ct + 1, at, :] += jnp.where(lane >= s, t1, t0)
                field[ct + 2, at, :] += jnp.where(lane < s, t1, 0.0)

        return carry

    lax.fori_loop(0, spots.shape[0] // 3, spot, 0)
    for k in range(EXT_TILES):
        weight[k] = 1.0 / (field[W // LANES + k, W : W + TILE, :] + SPECIMEN_REG)


def light(spots, probe):
    return pl.pallas_call(
        light_kernel,
        out_shape=pltpu.HBM((EXT_TILES, TILE, LANES), F32),
        in_specs=[SMEM, VMEM],
        out_specs=VMEM,
        scratch_shapes=[pltpu.VMEM((W, W), F32), pltpu.VMEM((PAD_TILES, PAD_ROWS, LANES), F32)],
        compiler_params=pltpu.CompilerParams(vmem_limit_bytes=12 << 20),
        cost_estimate=pl.CostEstimate(flops=20 << 20, bytes_accessed=20 << 20, transcendentals=0),
        name="light",
    )(spots, probe)


def shift(value, axis, by):
    length = lax.axis_size(axis)
    pairs = [(i, i + by) for i in range(length) if 0 <= i + by < length]
    return lax.ppermute(value, axis, pairs)


def sibling(value):
    return lax.ppermute(value, "ty", [(i, i ^ 1) for i in range(lax.axis_size("ty"))])


def in_hbm(value):
    return pltpu.with_memory_space_constraint(value, pltpu.HBM)


def exchange(value):
    rows, columns = lax.axis_size("ty"), lax.axis_size("tx")
    groups = [[i * columns + j for i in range(parity, rows, 2) for j in range(columns)] for parity in (0, 1)]
    return lax.all_to_all(value, BOTH, 0, 0, tiled=True, axis_index_groups=groups)


def probe_step(mine, probe):
    ty, tx = lax.axis_index("ty"), lax.axis_index("tx")
    half, chunk = ty % 2, (ty // 2) * lax.axis_size("tx") + tx
    mine = mine.reshape(CHUNKS, 16, LANES).sum(axis=0)
    start = (0, half * H + 4 * (chunk // 2), LANES * (chunk % 2))
    own = lax.dynamic_slice(probe, start, (2, 4, LANES)).reshape(8, LANES)
    denominator = mine[8:12] + PROBE_REG
    new = own + mine[0:8] / jnp.concatenate([denominator, denominator])
    return jnp.broadcast_to(new, (CHUNKS, 8, LANES)).reshape(CHUNKS * 8, LANES)


def edges(total, down, up, depth, split):
    def strip(lo, hi):
        parts = [total[:, lo:hi, :H] + down[:, lo:hi], total[:, lo:hi, H + W :] + up[:, lo:hi]]
        if not split:
            parts.insert(1, total[:, lo:hi, H : H + W])
        return jnp.concatenate(parts, axis=2)

    return strip(0, depth), strip(EXT_TILES - depth, EXT_TILES)


def finish(swept, probe, weight, mid_rows):
    total, _, u_top, u_bottom, s_left, s_right, keep, give = swept
    depth = s_left.shape[1]
    split = mid_rows is not None
    sums = (keep + sibling(give)).reshape(CHUNKS * 16, LANES)
    down = shift(u_bottom, "ty", 1)
    up = shift(u_top, "ty", -1)
    rows = ()
    if split:
        m_left = shift(s_right, "tx", 1)
        m_right = shift(s_left, "tx", -1)
        rows = mid_rows(total, weight, m_left, m_right)
    low, high = edges(total, down, up, depth, split)
    mine = exchange(sums)
    low, high, mine, rows, weight = lax.optimization_barrier((low, high, mine, rows, weight))
    e_left = shift(high, "tx", 1)
    e_right = shift(low, "tx", -1)
    chunks = exchange(probe_step(mine, probe))
    e_left, e_right, chunks = lax.optimization_barrier((e_left, e_right, chunks))
    chunks = chunks.reshape(CHUNKS, 8, LANES)
    return (chunks, sibling(chunks)), (total, down, up, e_left, e_right), weight, rows


def body(specimen, probe_field, intensity, positions, occupied_slots):
    ty, tx = lax.axis_index("ty"), lax.axis_index("tx")
    row_start = ty * TILE - H
    column_start = tx * TILE - H
    corners = positions - jnp.stack([row_start, column_start])[None, :]
    tables = jnp.asarray(dft_tables())
    half = (ty % 2).reshape(1)
    alive = jnp.concatenate([occupied_slots, half])

    slots = jnp.concatenate([positions, occupied_slots[:, None]], axis=1).astype(F32)
    tag = jnp.pad(slots, ((0, 0), (0, LANES - 3)))
    both = jnp.broadcast_to(tag, (2, SLOTS, LANES))
    left = shift(jnp.concatenate([specimen[:, :, TILE - H :], both], axis=1), "tx", 1)
    right = shift(jnp.concatenate([specimen[:, :, :H], both], axis=1), "tx", -1)
    top = shift(specimen[:, TILE - H :, :], "ty", 1)
    bottom = shift(specimen[:, :H, :], "ty", -1)
    amp = prepare(intensity)
    left, right, top, bottom, amp = lax.optimization_barrier((left, right, top, bottom, amp))
    sides = jnp.stack([left, right])
    tags = jnp.stack([sides[:, 0, TILE:, :], both], axis=1)
    corner_top = shift(jnp.concatenate([sides[:, :, TILE - H : TILE, :], tags], axis=2), "ty", 1)
    corner_bottom = shift(jnp.concatenate([sides[:, :, :H, :], tags], axis=2), "ty", -1)

    objects = (in_hbm(specimen), left, right, top, bottom, corner_top, corner_bottom)
    swept = sweep(True, corners, alive, objects, (probe_field,), amp, tables)

    lines = [x[:, :, -SLOTS:, :3].reshape(4, SLOTS, 3)[:3] for x in (corner_top, tags, corner_bottom)]
    around = jnp.concatenate(lines).reshape(9 * SLOTS, 3).astype(jnp.int32)
    spots = (around - jnp.stack([ty * TILE - W, column_start - W, 0])[None, :]).reshape(-1)
    weight = light(spots, probe_field)


    def mid_rows(total, weight, m_left, m_right):
        return rows_step(
            mid_rows_kernel, (1, 2), specimen, left, right, total, weight, (m_left, m_right), (), "mid_rows"
        )

    chunks, terms, weight, mid = finish(swept, probe_field, weight, mid_rows)
    total, down, up, e_left, e_right = terms
    first_rows, last_rows = rows_step(
        edge_rows_kernel, (0, 3), specimen, left, right, total, weight, (e_left, e_right), (down, up), "edge_rows"
    )
    top = shift(last_rows, "ty", 1)
    bottom = shift(first_rows, "ty", -1)
    rows = (first_rows, *mid, last_rows)

    swept = sweep(False, corners, alive, tuple(in_hbm(x) for x in rows) + (top, bottom), chunks, amp, tables)
    probe_field = swept[1]
    weight = light(spots, probe_field)
    chunks, terms, weight, _ = finish(swept, probe_field, weight, None)
    return last_step(half, chunks, rows, terms, weight)


def solution(mesh):
    return jax.shard_map(
        body,
        mesh=mesh,
        in_specs=(
            P(None, "ty", "tx"),
            P(),
            P(BOTH, None, None),
            P(BOTH, None),
            P(BOTH),
        ),
        out_specs=(P(None, "ty", "tx"), P()),
        check_vma=False,
    )
```

```python
import functools
import math

import jax
import jax.numpy as jnp
import numpy as np
from jax import lax
from jax.experimental import pallas as pl
from jax.experimental.pallas import tpu as pltpu
from jax.sharding import PartitionSpec as P

FLOOR = 0.2
SPECIMEN_REG = 0.5
PROBE_REG = 1.0

W = 256
H = W // 2
TILE = 512
EXT = TILE + 2 * H
SLOTS = 8
LANES = 128
EXT_TILES = EXT // LANES
CHUNKS = 64
BOTH = ("ty", "tx")
F32 = jnp.float32
BF16 = jnp.bfloat16
VMEM = pl.BlockSpec(memory_space=pltpu.VMEM)
SMEM = pl.BlockSpec(memory_space=pltpu.SMEM)


def dft_tables():
    j = np.arange(H)[:, None]
    m = np.arange(H)[None, :]
    parts = []
    for odd in (0, 1):
        phase = -2.0 * np.pi * ((m * (2 * j + odd)) % W) / W
        re, im = np.cos(phase) / math.sqrt(W), np.sin(phase) / math.sqrt(W)
        full = np.block([[re, -im], [im, re]])
        for mat in (full, full.T):
            hi = mat.astype(jnp.bfloat16)
            lo = (mat - hi.astype(np.float64)).astype(jnp.bfloat16)
            parts.append(np.stack([hi, lo]))
    return np.stack(parts)


def column_order():
    pick = np.zeros((W, W), np.float32)
    for k in range(H):
        pick[2 * k, k] = 1.0
        pick[2 * k + 1, H + k] = 1.0
    return pick.astype(jnp.bfloat16)


def split2(x):
    hi = x.astype(BF16)
    return hi, (x - hi.astype(F32)).astype(BF16)


def dot(a, b):
    return jnp.dot(a, b, preferred_element_type=F32)


def split3(x):
    hi = x.astype(BF16)
    return (hi,) + split2(x - hi.astype(F32))


def prep_kernel(intensity, pick, pick_t, amp):
    def slot(p, carry):
        hi, mid, lo = split3(jnp.sqrt(intensity[p]))
        x = dot(lo, pick[...]) + dot(mid, pick[...]) + dot(hi, pick[...])
        hi, mid, lo = split3(x)
        amp[p] = dot(pick_t[...], lo) + dot(pick_t[...], mid) + dot(pick_t[...], hi)
        return carry

    lax.fori_loop(0, SLOTS, slot, 0)


def prepare(intensity):
    pick = column_order()
    return pl.pallas_call(
        prep_kernel,
        out_shape=pltpu.HBM((SLOTS, W, W), F32),
        in_specs=[VMEM, VMEM, VMEM],
        out_specs=VMEM,
        cost_estimate=pl.CostEstimate(flops=4 * 3 * SLOTS * W**3, bytes_accessed=16 * SLOTS * W * W, transcendentals=SLOTS * W * W),
        name="amplitudes",
    )(intensity, jnp.asarray(pick), jnp.asarray(pick.T))


def run_copies(pairs, sems):
    copies = [pltpu.make_async_copy(src, dst, sems.at[n]) for n, (src, dst) in enumerate(pairs)]
    for copy in copies:
        copy.start()
    return copies


def first_loads(refs, ext):
    tile, left, right, top, bottom, corner_top, corner_bottom = refs
    inner, upper, lower = pl.ds(H, TILE), pl.ds(0, H), pl.ds(H + TILE, H)
    last = EXT_TILES - 1
    pairs = [
        (left.at[:, pl.ds(0, TILE)], ext.at[:, 0, inner]),
        (right.at[:, pl.ds(0, TILE)], ext.at[:, last, inner]),
        (corner_top.at[:, 0, pl.ds(0, H)], ext.at[:, 0, upper]),
        (corner_top.at[:, 1, pl.ds(0, H)], ext.at[:, last, upper]),
        (corner_bottom.at[:, 0, pl.ds(0, H)], ext.at[:, 0, lower]),
        (corner_bottom.at[:, 1, pl.ds(0, H)], ext.at[:, last, lower]),
    ]
    for k in range(TILE // LANES):
        cs = pl.ds(k * LANES, LANES)
        pairs.append((tile.at[:, :, cs], ext.at[:, 1 + k, inner]))
        pairs.append((top.at[:, :, cs], ext.at[:, 1 + k, upper]))
        pairs.append((bottom.at[:, :, cs], ext.at[:, 1 + k, lower]))
    return pairs


def later_loads(refs, ext):
    *rows, top, bottom = refs
    return [(x, ext.at[:, :, pl.ds(H * (n + 1), H)]) for n, x in enumerate(rows)] + [
        (top, ext.at[:, :, pl.ds(0, H)]),
        (bottom, ext.at[:, :, pl.ds(H + TILE, H)]),
    ]


FIRST_COPIES = 18
LATER_COPIES = 6


def unpack_probe(halves, probe):
    for h, chunks in enumerate(halves):
        for k in range(CHUNKS):
            rows = pl.ds(h * H + 4 * (k // 2), 4)
            cs = pl.ds((k % 2) * LANES, LANES)
            probe[0, rows, cs] = chunks[k, 0:4, :]
            probe[1, rows, cs] = chunks[k, 4:8, :]


def sweep_kernel(first, corners, alive, *refs):
    n, m = (7, 1) if first else (6, 2)
    objects, probe_in, (amp_in, tables_in) = refs[:n], refs[n : n + m], refs[n + m : n + m + 2]
    rest = refs[n + m + 2 :]
    half = alive[SLOTS]
    u_mid, probe, u_top, u_bottom, s_left, s_right, keep, give = rest[:8]
    total, ext, pack, amp, tables, windows, exit_waves, grads, his, los, wides, ext_sems, amp_sems, sems, out_sems, halves = rest[8:]
    loads = first_loads if first else later_loads
    copies = run_copies(loads(objects, ext), ext_sems)
    more = [(tables_in, tables)]
    if first:
        more.append((probe_in[0], probe))
    else:
        more += [(probe_in[0], halves.at[half]), (probe_in[1], halves.at[1 - half])]
    copies += run_copies(more, sems)
    run_copies([(amp_in.at[p], amp.at[p]) for p in range(SLOTS)], amp_sems)
    total[...] = jnp.zeros_like(total)
    grads[...] = jnp.zeros_like(grads)
    even, even_t, odd, odd_t = 0, 1, 2, 3
    step = 16
    lane = lax.broadcasted_iota(jnp.int32, (step, LANES), 1)
    for copy in copies:
        copy.wait()
    if not first:
        unpack_probe((halves.at[0], halves.at[1]), probe)

    def slot(p, z):
        window, exit_wave = windows.at[z], exit_waves.at[z]
        a_hi, a_lo, wide = his.at[z], los.at[z], wides.at[z]

        def left_dot(t, branch):
            rows = pl.ds(branch * W, W)
            hi, lo = a_hi[rows, :], a_lo[rows, :]
            wide[rows, :] = dot(tables[t, 0], hi) + dot(tables[t, 1], hi) + dot(tables[t, 0], lo)

        def right_dot(t, branch):
            rows = pl.ds(branch * W, W)
            hi, lo = a_hi[rows, :], a_lo[rows, :]
            wide[rows, :] = dot(hi, tables[t, 0]) + dot(hi, tables[t, 1]) + dot(lo, tables[t, 0])

        def put(row, col, value):
            hi, lo = split2(value)
            a_hi[pl.ds(row, step), pl.ds(col, LANES)] = hi
            a_lo[pl.ds(row, step), pl.ds(col, LANES)] = lo

        live = alive[p].astype(F32)
        r = corners[p, 0]
        c = corners[p, 1]
        ct = jnp.minimum(c // LANES, EXT_TILES - 3)
        s = c - ct * LANES
        back_turn = lax.rem(LANES - s, LANES)
        forth_turn = lax.rem(s, LANES)

        for i in range(0, H, step):
            waves = []
            for half in (0, 1):
                parts = []
                for plane in (0, 1):
                    turned = [
                        pltpu.roll(ext[plane, ct + k, pl.ds(r + half * H + i, step), :], back_turn, 1)
                        for k in range(3)
                    ]
                    cols = [jnp.where(lane < LANES - s, turned[k], turned[k + 1]) for k in (0, 1)]
                    parts.append(cols)
                rows = pl.ds(half * H + i, step)
                wave = []
                for k in (0, 1):
                    cs = pl.ds(k * LANES, LANES)
                    o_re, o_im = parts[0][k], parts[1][k]
                    p_re, p_im = probe[0, rows, cs], probe[1, rows, cs]
                    w_re = p_re * o_re - p_im * o_im
                    w_im = p_re * o_im + p_im * o_re
                    window[0, rows, cs] = o_re
                    window[1, rows, cs] = o_im
                    exit_wave[0, rows, cs] = w_re
                    exit_wave[1, rows, cs] = w_im
                    wave.append((w_re, w_im))
                waves.append(wave)
            for k in (0, 1):
                for part in (0, 1):
                    x0, x1 = waves[0][k][part], waves[1][k][part]
                    put(part * H + i, k * LANES, x0 + x1)
                    put(W + part * H + i, k * LANES, x0 - x1)
        left_dot(even, 0)
        left_dot(odd, 1)
        yield

        for branch in (0, 1):
            for i in range(0, H, step):
                for part in (0, 1):
                    rows = pl.ds(branch * W + part * H + i, step)
                    x0, x1 = wide[rows, 0:LANES], wide[rows, LANES:W]
                    put(branch * H + i, part * LANES, x0 + x1)
                    put(W + branch * H + i, part * LANES, x0 - x1)
        right_dot(even_t, 0)
        right_dot(odd_t, 1)
        yield

        for branch in (0, 1):
            for i in range(0, W, step):
                rows = pl.ds(branch * W + i, step)
                z_re, z_im = wide[rows, 0:LANES], wide[rows, LANES:W]
                power = z_re * z_re + z_im * z_im
                factor = amp[p, pl.ds(i, step), pl.ds(branch * LANES, LANES)] * lax.rsqrt(
                    jnp.maximum(power, FLOOR * FLOOR)
                )
                put(branch * W + i, 0, z_re * factor)
                put(branch * W + i, LANES, z_im * factor)
        right_dot(even, 0)
        right_dot(odd, 1)
        yield

        for branch in (0, 1):
            for i in range(0, H, step):
                rows_e = pl.ds(branch * H + i, step)
                rows_o = pl.ds(W + branch * H + i, step)
                for part in (0, 1):
                    cs = pl.ds(part * LANES, LANES)
                    x0, x1 = wide[rows_e, cs], wide[rows_o, cs]
                    put(branch * W + part * H + i, 0, x0 + x1)
                    put(branch * W + part * H + i, LANES, x0 - x1)
        left_dot(even_t, 0)
        left_dot(odd_t, 1)
        yield

        for i in range(0, H, step):
            for half in (0, 1):
                rows = pl.ds(half * H + i, step)
                turned = [[], []]
                for k in (0, 1):
                    cs = pl.ds(k * LANES, LANES)
                    back = []
                    for part in (0, 1):
                        x0 = wide[pl.ds(part * H + i, step), cs]
                        x1 = wide[pl.ds(W + part * H + i, step), cs]
                        back.append(x0 + x1 if half == 0 else x0 - x1)
                    d_re = live * (back[0] - exit_wave[0, rows, cs])
                    d_im = live * (back[1] - exit_wave[1, rows, cs])
                    o_re, o_im = window[0, rows, cs], window[1, rows, cs]
                    grads[0, rows, cs] += o_re * d_re + o_im * d_im
                    grads[1, rows, cs] += o_re * d_im - o_im * d_re
                    grads[2, rows, cs] += live * (o_re * o_re + o_im * o_im)
                    p_re, p_im = probe[0, rows, cs], probe[1, rows, cs]
                    turned[0].append(pltpu.roll(p_re * d_re + p_im * d_im, forth_turn, 1))
                    turned[1].append(pltpu.roll(p_re * d_im - p_im * d_re, forth_turn, 1))
                at = pl.ds(r + half * H + i, step)
                for part in (0, 1):
                    t0, t1 = turned[part]
                    total[part, ct, at, :] += jnp.where(lane >= s, t0, 0.0)
                    total[part, ct + 1, at, :] += jnp.where(lane >= s, t1, t0)
                    total[part, ct + 2, at, :] += jnp.where(lane < s, t1, 0.0)

    def pair(q, carry):
        for z in (0, 1):
            pltpu.make_async_copy(amp_in.at[2 * q + z], amp.at[2 * q + z], amp_sems.at[2 * q + z]).wait()

        @pl.when((alive[2 * q] != 0) | (alive[2 * q + 1] != 0))
        def _():
            runs = [slot(2 * q, 0), slot(2 * q + 1, 1)]
            for _ in range(5):
                for run in runs:
                    next(run, None)

        return carry

    lax.fori_loop(0, SLOTS // 2, pair, 0)
    depth = s_left.shape[1]
    mid = pl.ds(2 * H, W)
    outs = run_copies(
        [
            (total.at[:, :, pl.ds(H + TILE, H)], u_bottom),
            (total.at[:, :, pl.ds(0, H)], u_top),
            (total.at[:, pl.ds(EXT_TILES - depth, depth), mid], s_right),
            (total.at[:, pl.ds(0, depth), mid], s_left),
            (total.at[:, :, pl.ds(H, TILE)], u_mid),
        ],
        out_sems,
    )
    for h in (0, 1):
        for k in range(CHUNKS):
            rows = pl.ds(h * H + 4 * (k // 2), 4)
            cs = pl.ds((k % 2) * LANES, LANES)
            for plane in range(3):
                pack[h, k, pl.ds(4 * plane, 4), :] = grads[plane, rows, cs]
            pack[h, k, pl.ds(12, 4), :] = jnp.zeros((4, LANES), F32)
    outs += run_copies([(pack.at[half], keep), (pack.at[1 - half], give)], sems)
    for copy in outs:
        copy.wait()


ANY = pl.BlockSpec(memory_space=pl.ANY)
HBM = pl.BlockSpec(memory_space=pltpu.HBM)


def sweep(first, corners, alive, objects, probe, amp, tables):
    flops = SLOTS * 24 * 2 * W**3
    depth = 2 if first else 1
    strip = pltpu.HBM((2, depth, W, LANES), F32)
    margin = pltpu.HBM((2, EXT_TILES, H, LANES), F32)
    whole = pltpu.VMEM((2, EXT_TILES, EXT, LANES), F32)
    return pl.pallas_call(
        functools.partial(sweep_kernel, first),
        out_shape=(
            pltpu.HBM((2, EXT_TILES, TILE, LANES), F32),
            jax.ShapeDtypeStruct((2, W, W), F32),
            margin,
            margin,
            strip,
            strip,
            pltpu.HBM((CHUNKS, 16, LANES), F32),
            pltpu.HBM((CHUNKS, 16, LANES), F32),
        ),
        in_specs=[SMEM, SMEM] + [HBM] * len(objects) + [HBM] * (len(probe) + 2),
        out_specs=(HBM, VMEM) + (HBM,) * 6,
        scratch_shapes=[
            whole,
            whole,
            pltpu.VMEM((2, CHUNKS, 16, LANES), F32),
            pltpu.VMEM((SLOTS, W, W), F32),
            pltpu.VMEM((4, 2, W, W), BF16),
            pltpu.VMEM((2, 2, W, W), F32),
            pltpu.VMEM((2, 2, W, W), F32),
            pltpu.VMEM((3, W, W), F32),
            pltpu.VMEM((2, 2 * W, W), BF16),
            pltpu.VMEM((2, 2 * W, W), BF16),
            pltpu.VMEM((2, 2 * W, W), F32),
            pltpu.SemaphoreType.DMA((FIRST_COPIES if first else LATER_COPIES,)),
            pltpu.SemaphoreType.DMA((SLOTS,)),
            pltpu.SemaphoreType.DMA((3,)),
            pltpu.SemaphoreType.DMA((5,)),
            pltpu.VMEM((2, CHUNKS, 8, LANES), F32),
        ],
        compiler_params=pltpu.CompilerParams(vmem_limit_bytes=28 << 20),
        cost_estimate=pl.CostEstimate(flops=flops, bytes_accessed=16 << 20, transcendentals=SLOTS * W * W),
        name="sweep",
    )(corners, alive, *objects, *probe, in_hbm(amp), in_hbm(tables))


ROWS = ((0, H), (H, H + W), (H + W, TILE))


def object_tile(base, total, down, up, weight, mid, edge, put):
    for plane in (0, 1):
        parts = [
            total[plane, 0, 0:H, :] + down[plane, 0],
            total[plane, 0, H : H + W, :],
            total[plane, 0, H + W : TILE, :] + up[plane, 0],
        ]
        if mid is not None:
            parts = [parts[0] + edge[plane, 0, 0:H, :], parts[1] + mid[plane, 0], parts[2] + edge[plane, 0, H:W, :]]
        elif edge is not None:
            parts = [parts[n] + edge[plane, 0, a:b, :] for n, (a, b) in enumerate(ROWS)]
        for n, (a, b) in enumerate(ROWS):
            put(plane, n, base(plane, a, b) + parts[n] * weight[0, a:b, :])


def rows_kernel(tiles, lefts, rights, totals, weights, s_left, s_right, folds, outs):
    k = pl.program_id(0)

    def run(bases, strip):
        for n in (0, 1):
            for plane in (0, 1):
                part = totals[n][plane, 0]
                if folds:
                    part = part + folds[n][plane, 0]
                if strip is not None:
                    part = part + strip[plane, 0, n * H : (n + 1) * H, :]
                outs[n][plane, 0] = bases[n][plane] + part * weights[n][0]

    last = EXT_TILES - 1
    pl.when(k == 0)(lambda: run(lefts, s_left))
    pl.when(k == 1)(lambda: run(tiles, s_left))
    pl.when((k > 1) & (k < last - 1))(lambda: run(tiles, None))
    pl.when(k == last - 1)(lambda: run(tiles, s_right))
    pl.when(k == last)(lambda: run(rights, s_right))


def edge_rows_kernel(t0, t1, l0, l1, r0, r1, u0, u1, w0, w1, s_left, s_right, down, up, o0, o1):
    rows_kernel((t0, t1), (l0, l1), (r0, r1), (u0, u1), (w0, w1), s_left, s_right, (down, up), (o0, o1))


def mid_rows_kernel(t0, t1, l0, l1, r0, r1, u0, u1, w0, w1, s_left, s_right, o0, o1):
    rows_kernel((t0, t1), (l0, l1), (r0, r1), (u0, u1), (w0, w1), s_left, s_right, (), (o0, o1))


def last_kernel(half, mine, other, m0, m1, m2, m3, total, down, up, e_left, e_right, weight, out, probe, halves):
    k = pl.program_id(0)

    @pl.when(k == 0)
    def _():
        halves[half[0]] = mine[...]
        halves[1 - half[0]] = other[...]
        unpack_probe((halves.at[0], halves.at[1]), probe)

    def put(plane, n, value):
        a, b = ROWS[n]
        out[plane, a:b, :] = value

    def base(plane, a, b):
        return jnp.concatenate([m[plane, 0] for m in (m0, m1, m2, m3)[a // H : b // H]], axis=0)

    def run(edge):
        object_tile(base, total, down, up, weight, None, edge, put)

    last = TILE // LANES - 1
    pl.when(k == 0)(lambda: run(e_left))
    pl.when((k > 0) & (k < last))(lambda: run(None))
    pl.when(k == last)(lambda: run(e_right))


def object_step(kernel, grid, in_specs, out_specs, out_shape, name, scratch, *args):
    return pl.pallas_call(
        kernel,
        grid=(grid,),
        out_shape=out_shape,
        in_specs=in_specs,
        out_specs=out_specs,
        scratch_shapes=scratch,
        compiler_params=pltpu.CompilerParams(vmem_limit_bytes=16 << 20),
        cost_estimate=pl.CostEstimate(flops=2 << 20, bytes_accessed=8 << 20, transcendentals=0),
        name=name,
    )(*args)


def tile_spec(rows, index, row=0):
    return pl.BlockSpec((2, 1, rows, LANES), lambda k: (0, index(k), row, 0))


def rows_step(kernel, blocks, specimen, left, right, total, weight, strips, folds, name):
    tiles = TILE // LANES
    specs = [pl.BlockSpec((2, H, LANES), lambda k, n=n: (0, n, jnp.clip(k - 1, 0, tiles - 1))) for n in blocks]
    specs += [pl.BlockSpec((2, H, LANES), lambda k, n=n: (0, n, 0)) for n in blocks] * 2
    specs += [tile_spec(H, lambda k: k, n) for n in blocks]
    specs += [pl.BlockSpec((1, H, LANES), lambda k, n=n: (k, n, 0)) for n in blocks]
    specs += [tile_spec(W, lambda k: jnp.minimum(k, 1)), tile_spec(W, lambda k: jnp.maximum(k - EXT_TILES + 2, 0))]
    specs += [tile_spec(H, lambda k: k) for _ in folds]
    specimen, total, weight = in_hbm(specimen), in_hbm(total), in_hbm(weight)
    return object_step(
        kernel,
        EXT_TILES,
        specs,
        (tile_spec(H, lambda k: k),) * 2,
        (pltpu.HBM((2, EXT_TILES, H, LANES), F32),) * 2,
        name,
        [],
        *[x for x in (specimen, left, right, total, weight) for _ in blocks],
        *strips,
        *folds,
    )


def last_step(half, chunks, rows, terms, weight):
    tiles = TILE // LANES
    total, *folds, e_left, e_right = terms
    whole = pl.BlockSpec((CHUNKS, 8, LANES), lambda k: (0, 0, 0))
    specs = [SMEM, whole, whole] + [tile_spec(H, lambda k: k + 1)] * 4 + [tile_spec(TILE, lambda k: k + 1)]
    specs += [tile_spec(H, lambda k: k + 1)] * 2 + [tile_spec(TILE, lambda k: 0)] * 2
    specs += [pl.BlockSpec((1, TILE, LANES), lambda k: (k + 1, 0, 0))]
    return object_step(
        last_kernel,
        tiles,
        specs,
        (pl.BlockSpec((2, TILE, LANES), lambda k: (0, 0, k)), pl.BlockSpec((2, W, W), lambda k: (0, 0, 0))),
        (jax.ShapeDtypeStruct((2, TILE, TILE), F32), jax.ShapeDtypeStruct((2, W, W), F32)),
        "last",
        [pltpu.VMEM((2, CHUNKS, 8, LANES), F32)],
        half,
        *chunks,
        *[in_hbm(x) for x in rows],
        in_hbm(total),
        *folds,
        e_left,
        e_right,
        in_hbm(weight),
    )


PAD_ROWS = TILE + 2 * W
PAD_TILES = (EXT + 2 * W) // LANES


def light_kernel(spots, probe, weight, density, field):
    density[...] = probe[0] * probe[0] + probe[1] * probe[1]
    field[...] = jnp.zeros_like(field)
    step = 16
    lane = lax.broadcasted_iota(jnp.int32, (step, LANES), 1)

    def spot(q, carry):
        r, c, on = spots[3 * q], spots[3 * q + 1], spots[3 * q + 2]

        @pl.when((on != 0) & (r > 0) & (r < W + TILE) & (c > 0) & (c < W + EXT))
        def _():
            ct = jnp.minimum(c // LANES, PAD_TILES - 3)
            s = c - ct * LANES
            turn = lax.rem(s, LANES)
            for i in range(0, W, step):
                at = pl.ds(r + i, step)
                t0 = pltpu.roll(density[pl.ds(i, step), 0:LANES], turn, 1)
                t1 = pltpu.roll(density[pl.ds(i, step), LANES:W], turn, 1)
                field[ct, at, :] += jnp.where(lane >= s, t0, 0.0)
                field[ct + 1, at, :] += jnp.where(lane >= s, t1, t0)
                field[ct + 2, at, :] += jnp.where(lane < s, t1, 0.0)

        return carry

    lax.fori_loop(0, spots.shape[0] // 3, spot, 0)
    for k in range(EXT_TILES):
        weight[k] = 1.0 / (field[W // LANES + k, W : W + TILE, :] + SPECIMEN_REG)


def light(spots, probe):
    return pl.pallas_call(
        light_kernel,
        out_shape=pltpu.HBM((EXT_TILES, TILE, LANES), F32),
        in_specs=[SMEM, VMEM],
        out_specs=VMEM,
        scratch_shapes=[pltpu.VMEM((W, W), F32), pltpu.VMEM((PAD_TILES, PAD_ROWS, LANES), F32)],
        compiler_params=pltpu.CompilerParams(vmem_limit_bytes=12 << 20),
        cost_estimate=pl.CostEstimate(flops=20 << 20, bytes_accessed=20 << 20, transcendentals=0),
        name="light",
    )(spots, probe)


def shift(value, axis, by):
    length = lax.axis_size(axis)
    pairs = [(i, i + by) for i in range(length) if 0 <= i + by < length]
    return lax.ppermute(value, axis, pairs)


def sibling(value):
    return lax.ppermute(value, "ty", [(i, i ^ 1) for i in range(lax.axis_size("ty"))])


def in_hbm(value):
    return pltpu.with_memory_space_constraint(value, pltpu.HBM)


def exchange(value):
    rows, columns = lax.axis_size("ty"), lax.axis_size("tx")
    groups = [[i * columns + j for i in range(parity, rows, 2) for j in range(columns)] for parity in (0, 1)]
    return lax.all_to_all(value, BOTH, 0, 0, tiled=True, axis_index_groups=groups)


def probe_step(mine, probe):
    ty, tx = lax.axis_index("ty"), lax.axis_index("tx")
    half, chunk = ty % 2, (ty // 2) * lax.axis_size("tx") + tx
    mine = mine.reshape(CHUNKS, 16, LANES).sum(axis=0)
    start = (0, half * H + 4 * (chunk // 2), LANES * (chunk % 2))
    own = lax.dynamic_slice(probe, start, (2, 4, LANES)).reshape(8, LANES)
    denominator = mine[8:12] + PROBE_REG
    new = own + mine[0:8] / jnp.concatenate([denominator, denominator])
    return jnp.broadcast_to(new, (CHUNKS, 8, LANES)).reshape(CHUNKS * 8, LANES)


def edges(total, down, up, depth, split):
    def strip(lo, hi):
        parts = [total[:, lo:hi, :H] + down[:, lo:hi], total[:, lo:hi, H + W :] + up[:, lo:hi]]
        if not split:
            parts.insert(1, total[:, lo:hi, H : H + W])
        return jnp.concatenate(parts, axis=2)

    return strip(0, depth), strip(EXT_TILES - depth, EXT_TILES)


def finish(swept, probe, weight):
    total, _, u_top, u_bottom, s_left, s_right, keep, give = swept
    depth = s_left.shape[1]
    split = depth > 1
    sums = (keep + sibling(give)).reshape(CHUNKS * 16, LANES)
    down = shift(u_bottom, "ty", 1)
    up = shift(u_top, "ty", -1)
    m_left = shift(s_right, "tx", 1) if split else None
    m_right = shift(s_left, "tx", -1) if split else None
    mine = exchange(sums)
    down, up, m_left, m_right, mine, weight = lax.optimization_barrier((down, up, m_left, m_right, mine, weight))
    low, high = edges(total, down, up, depth, split)
    e_left = shift(high, "tx", 1)
    e_right = shift(low, "tx", -1)
    chunks = exchange(probe_step(mine, probe))
    chunks = chunks.reshape(CHUNKS, 8, LANES)
    e_left, e_right, chunks, other = lax.optimization_barrier((e_left, e_right, chunks, sibling(chunks)))
    strips = (m_left, m_right, e_left, e_right) if split else (e_left, e_right)
    return (chunks, other), (total, down, up) + strips, weight


def body(specimen, probe_field, intensity, positions, occupied_slots):
    ty, tx = lax.axis_index("ty"), lax.axis_index("tx")
    row_start = ty * TILE - H
    column_start = tx * TILE - H
    corners = positions - jnp.stack([row_start, column_start])[None, :]
    tables = jnp.asarray(dft_tables())
    half = (ty % 2).reshape(1)
    alive = jnp.concatenate([occupied_slots, half])

    slots = jnp.concatenate([positions, occupied_slots[:, None]], axis=1).astype(F32)
    tag = jnp.pad(slots, ((0, 0), (0, LANES - 3)))
    both = jnp.broadcast_to(tag, (2, SLOTS, LANES))
    left = shift(jnp.concatenate([specimen[:, :, TILE - H :], both], axis=1), "tx", 1)
    right = shift(jnp.concatenate([specimen[:, :, :H], both], axis=1), "tx", -1)
    top = shift(specimen[:, TILE - H :, :], "ty", 1)
    bottom = shift(specimen[:, :H, :], "ty", -1)
    amp = prepare(intensity)
    left, right, top, bottom, amp = lax.optimization_barrier((left, right, top, bottom, amp))
    sides = jnp.stack([left, right], axis=1)
    tags = jnp.stack([sides[0, :, TILE:, :], both])
    corner_top = shift(jnp.concatenate([sides[:, :, TILE - H : TILE, :], tags], axis=2), "ty", 1)
    corner_bottom = shift(jnp.concatenate([sides[:, :, :H, :], tags], axis=2), "ty", -1)

    objects = (in_hbm(specimen), left, right, top, bottom, corner_top, corner_bottom)
    swept = sweep(True, corners, alive, objects, (probe_field,), amp, tables)

    lines = [x[:, :, -SLOTS:, :3].reshape(4, SLOTS, 3)[:3] for x in (corner_top, tags, corner_bottom)]
    around = jnp.concatenate(lines).reshape(9 * SLOTS, 3).astype(jnp.int32)
    spots = (around - jnp.stack([ty * TILE - W, column_start - W, 0])[None, :]).reshape(-1)
    weight = light(spots, probe_field)

    chunks, terms, weight = finish(swept, probe_field, weight)
    total, down, up, m_left, m_right, e_left, e_right = terms
    first_rows, last_rows = rows_step(
        edge_rows_kernel, (0, 3), specimen, left, right, total, weight, (e_left, e_right), (down, up), "edge_rows"
    )
    top = shift(last_rows, "ty", 1)
    bottom = shift(first_rows, "ty", -1)
    mid_rows = rows_step(
        mid_rows_kernel, (1, 2), specimen, left, right, total, weight, (m_left, m_right), (), "mid_rows"
    )
    rows = (first_rows, *mid_rows, last_rows)

    swept = sweep(False, corners, alive, tuple(in_hbm(x) for x in rows) + (top, bottom), chunks, amp, tables)
    probe_field = swept[1]
    weight = light(spots, probe_field)
    chunks, terms, weight = finish(swept, probe_field, weight)
    return last_step(half, chunks, rows, terms, weight)


def solution(mesh):
    return jax.shard_map(
        body,
        mesh=mesh,
        in_specs=(
            P(None, "ty", "tx"),
            P(),
            P(BOTH, None, None),
            P(BOTH, None),
            P(BOTH),
        ),
        out_specs=(P(None, "ty", "tx"), P()),
        check_vma=False,
    )
```
